32 devices in a mesh: grp: 2 (over x), lat: 8 (over z, y), lon: 2 (over core).
Axes of the slice: x: 2, y: 2, z: 4, core: 2. Of those that a mesh axis runs over, the one named last changes fastest.
Arguments:
- perturb: float32 [256, 256, 192], P(('grp', 'lat'), 'lon'), parts along dimension 0, may hold values from -110 to 110, as said below
- kernels: float32 [2, 7, 7, 192], replicated, may hold values from -0.875 to 0.875
- gains: float32 [2, 192], replicated, may hold values from 0.5 to 1.5
- w_in: bfloat16 [2, 192, 768], replicated, may hold values from -0.4375 to 0.4375
- w_out: bfloat16 [2, 768, 192], replicated, may hold values from -0.21875 to 0.21875
- scales: float32 [2, 192], replicated, may hold values from 0.3 to 1.5
- normed: bfloat16 [2, 256, 256, 192], P(None, ('grp', 'lat'), 'lon'), parts along dimension 1, may hold values from -6 to 6
- inv_std: float32 [2, 256, 256], P(None, ('grp', 'lat'), 'lon'), parts along dimension 1, may hold values from 0.5 to 2
- slope: bfloat16 [2, 256, 256, 768], P(None, ('grp', 'lat'), 'lon'), parts along dimension 1, may hold values from -0.099609375 to 1.09375
Outputs:
- new_vec: float32 [256, 256, 192], P(('grp', 'lat'), 'lon'), parts along dimension 0
- growth: float32 [2], P('grp'), parts along dimension 0
The draws below stay inside these ranges and needn't reach their ends.
There are 2 independent parts, one for each index of `grp`. The reference program is written for one: setup_inputs(seed, part) draws one part's arguments, and reference() takes and returns one part's arrays. A program takes and returns all parts, laid end to end along the dimension named above; an argument that names none is the same for every part. Nothing has to cross between parts.
Inputs may be any that keep to these rules, and one draw needn't show every extreme that they name: `perturb`: the initial perturbation.
All inputs are finite; a program needn't handle non-finite values.
Results may differ from the reference program's by a relative error of at most 0.0075.
Values may be sent and summed in bfloat16 or wider, within the bound.
No kernel may reach another device: no remote copies, remote signals or barrier semaphores. Data moves between devices by JAX's collectives and lax.ppermute only.
A program may use at most 64 MiB of HBM per device.

```python
import math
import jax
import jax.numpy as jnp
from jax import lax

C = 192
HID = 768
LAYERS = 2
NLAT = 128
NLON = 256


def draw_perturb(key, part):
    raw_key, row_key, chan_key = jax.random.split(jax.random.fold_in(key, 11), 3)
    raw_values = jnp.clip(jax.random.normal(raw_key, (NLAT, NLON, C), jnp.float32), -6.0, 6.0)
    row_span = math.log(10.0)
    row_scale = jnp.exp(jax.random.uniform(row_key, (NLAT, 1, 1), jnp.float32) * row_span)
    chan_scale = jnp.exp(jax.random.uniform(chan_key, (1, 1, C), jnp.float32) * math.log(10.0))
    return (raw_values * row_scale * chan_scale / 10.0).astype(jnp.float32)


def shard_levels(key, extent, cuts, least, top_value):
    level, own = 1.0, jax.random.fold_in(key, 6)
    for position, shards_of in cuts:
        heights = jnp.exp(jax.random.uniform(jax.random.fold_in(own, position), (shards_of,), jnp.float32, least / len(cuts), top_value / len(cuts)))
        level = level * jnp.repeat(heights, extent[position] // shards_of).reshape([-1 if axis == position else 1 for axis in range(len(extent))])
    return level


def noise(rng, shape, deviation, most, cuts=(), held_as=jnp.bfloat16):
    drawn = jax.random.normal(rng, shape, jnp.float32) * deviation
    if len(cuts) > 0:
        drawn = shard_levels(rng, shape, cuts, -0.22, 0.18) * drawn
    return jnp.clip(drawn, min=-most, max=most).astype(held_as)


def setup_inputs(seed: int = 0, part: int = 0) -> dict:
    key_list = jax.random.split(jax.random.key(seed), 10)
    part_keys = jax.random.split(jax.random.fold_in(key_list[9], part), 10)
    return {
        "perturb": draw_perturb(jax.random.fold_in(jax.random.fold_in(key_list[9], part), 71), part),
        "kernels": noise(key_list[1], (LAYERS, 7, 7, C), 49 ** -0.5, 0.875, (), jnp.float32),
        "gains": jnp.clip(1.0 + 0.1 * jax.random.normal(key_list[2], (LAYERS, C), jnp.float32), 0.5, 1.5),
        "w_in": noise(key_list[3], (LAYERS, C, HID), C ** -0.5, 0.4375),
        "w_out": noise(key_list[4], (LAYERS, HID, C), HID ** -0.5, 0.21875),
        "scales": jnp.clip(jnp.exp(jax.random.uniform(key_list[5], (LAYERS, C), jnp.float32, math.log(0.3), math.log(1.5))), 0.3, 1.5),
        "normed": noise(part_keys[6], (LAYERS, NLAT, NLON, C), 1.0, 6.0, ((1, 8), (2, 2))),
        "inv_std": jnp.clip(jnp.exp(math.log(2.0) - 1.3862944 * jax.random.uniform(part_keys[7], (LAYERS, NLAT, NLON), jnp.float32) ** shard_levels(part_keys[7], (LAYERS, NLAT, NLON), ((1, 8), (2, 2)), -0.2, 0.2)), 0.5, 2.0),
        "slope": jnp.clip(-0.099609375 + 1.1933594 * jax.random.uniform(part_keys[8], (LAYERS, NLAT, NLON, HID), jnp.float32) ** shard_levels(part_keys[8], (LAYERS, NLAT, NLON, HID), ((1, 8), (2, 2)), -0.2, 0.2), -0.099609375, 1.09375).astype(jnp.bfloat16),
    }


lat_span = 70.0 * math.pi / 180.0

def pad_grid(field):
    padded = jnp.pad(field, ((3, 3), (0, 0), (0, 0)))
    return jnp.concatenate([padded[:, -3:], padded, padded[:, :3]], axis=1)

def conv_forward(field, kernel):
    padded = pad_grid(field)
    row_count, col_count = (field.shape[0], field.shape[1])
    summed = jnp.zeros(field.shape, jnp.float32)
    for row_off in range(7):
        for col_off in range(7):
            summed = summed + kernel[row_off, col_off] * padded[row_off:row_off + row_count, col_off:col_off + col_count]
    return summed

def conv_adjoint(field, kernel):
    padded = pad_grid(field)
    row_count, col_count = (field.shape[0], field.shape[1])
    summed = jnp.zeros(field.shape, jnp.float32)
    for row_off in range(7):
        for col_off in range(7):
            summed = summed + kernel[row_off, col_off] * padded[6 - row_off:6 - row_off + row_count, 6 - col_off:6 - col_off + col_count]
    return summed

def project(values, normed_layer, inv_layer):
    normal_f = normed_layer.astype(jnp.float32)
    centred = values - lax.optimization_barrier(jnp.mean(values, axis=-1, keepdims=True)) - normal_f * lax.optimization_barrier(jnp.mean(normal_f * values, axis=-1, keepdims=True))
    return inv_layer[..., None] * centred

def reference(perturb, kernels, gains, w_in, w_out, scales, normed, inv_std, slope):
    rows_f = jnp.arange(NLAT).astype(jnp.float32)
    area_rows = jnp.cos(lat_span * (rows_f + 0.5) / NLAT)
    area_w = area_rows[:, None, None]
    weight_total = jnp.sum(area_rows) * NLON * C
    tangent = perturb
    for layer_index in range(LAYERS):
        rounded = tangent.astype(jnp.bfloat16)
        conv_out = conv_forward(rounded.astype(jnp.float32), kernels[layer_index])
        tangent_norm = project(conv_out, normed[layer_index], inv_std[layer_index])
        operand = (gains[layer_index] * tangent_norm).astype(jnp.bfloat16)
        hidden_pre = jnp.dot(operand, w_in[layer_index], preferred_element_type=jnp.float32)
        gated = (slope[layer_index].astype(jnp.float32) * hidden_pre).astype(jnp.bfloat16)
        branch_out = jnp.dot(gated, w_out[layer_index], preferred_element_type=jnp.float32)
        tangent = tangent + scales[layer_index] * branch_out
    forward_out = tangent
    grad_field = area_w * forward_out
    for layer_index in range(LAYERS - 1, -1, -1):
        scaled = (scales[layer_index] * grad_field).astype(jnp.bfloat16)
        hidden_back = lax.dot_general(scaled, w_out[layer_index], (((2,), (1,)), ((), ())), preferred_element_type=jnp.float32)
        gated = (slope[layer_index].astype(jnp.float32) * hidden_back).astype(jnp.bfloat16)
        chan_back = lax.dot_general(gated, w_in[layer_index], (((2,), (1,)), ((), ())), preferred_element_type=jnp.float32)
        conv_grad = project(gains[layer_index] * chan_back, normed[layer_index], inv_std[layer_index]).astype(jnp.bfloat16)
        grad_field = grad_field + conv_adjoint(conv_grad.astype(jnp.float32), kernels[layer_index])
    adjoint_out = grad_field / area_w
    start_sq = jnp.sum(area_w * perturb * perturb) / weight_total
    forward_sq = jnp.sum(area_w * forward_out * forward_out) / weight_total
    adjoint_sq = jnp.sum(area_w * adjoint_out * adjoint_out) / weight_total
    growth = jnp.sqrt(forward_sq / (start_sq + 1e-06)).reshape(1)
    new_vec = adjoint_out / jnp.sqrt(adjoint_sq + 1e-06)
    return (new_vec, growth)
```

```python
import functools
import math

import jax
import jax.numpy as jnp
import numpy as np
from jax import lax
from jax.experimental import pallas as pl
from jax.experimental.pallas import tpu as pltpu
from jax.sharding import PartitionSpec as P

F32 = jnp.float32
BF16 = jnp.bfloat16
LAT_SPAN = 70.0 * math.pi / 180.0
MARGIN = 8
EXT = 8
VMEM = pltpu.VMEM
IN_VMEM = pl.BlockSpec(memory_space=pltpu.VMEM)
IN_SMEM = pl.BlockSpec(memory_space=pltpu.SMEM)


def in_vmem(x):
    return pltpu.with_memory_space_constraint(x, pltpu.VMEM)


def tap_index(a, b, flipped):
    return (6 - a) * 7 + (6 - b) if flipped else a * 7 + b


def fill_taps(taps_ref, layer, low_scr, high_scr):
    for i in range(49):
        row = taps_ref[layer, i // 7, i % 7 : i % 7 + 1, :]
        low_scr[i] = jnp.broadcast_to(row[:, :128], (8, 128))
        high = jnp.broadcast_to(row[:, 128:], (8, row.shape[1] - 128))
        high_scr[i] = jnp.concatenate([high, high], axis=1)


def conv_local(load_row, lon_ref, taps_ref, layer, out_ref, xs0, xs1, k0, k1, flipped):
    rows, cols, _ = out_ref.shape
    half = rows // 2
    fill_taps(taps_ref, layer, k0, k1)
    zero = jnp.zeros((cols + 2 * MARGIN, 64), F32)

    @pl.loop(0, rows)
    def _(r):
        xs0[r, MARGIN : MARGIN + cols, :] = load_row(r)[:, :128]
        side = lon_ref[r].astype(F32)
        xs0[r, MARGIN - 3 : MARGIN, :] = side[0:3, :128]
        xs0[r, MARGIN + cols : MARGIN + cols + 3, :] = side[3:6, :128]

    def high_part(r):
        side = lon_ref[r].astype(F32)
        return load_row(r)[:, 128:], side[0:3, 128:], side[3:6, 128:]

    @pl.loop(0, half)
    def _(r):
        low, high = high_part(r), high_part(r + half)
        both = [jnp.concatenate([x, y], axis=1) for x, y in zip(low, high)]
        xs1[r + 3, MARGIN : MARGIN + cols, :] = both[0]
        xs1[r + 3, MARGIN - 3 : MARGIN, :] = both[1]
        xs1[r + 3, MARGIN + cols : MARGIN + cols + 3, :] = both[2]

    @pl.loop(0, 3)
    def _(q):
        mid, left, right = high_part(q + half - 3)
        xs1[q, MARGIN : MARGIN + cols, :] = jnp.concatenate([zero[:cols], mid], axis=1)
        xs1[q, MARGIN - 3 : MARGIN, :] = jnp.concatenate([zero[:3], left], axis=1)
        xs1[q, MARGIN + cols : MARGIN + cols + 3, :] = jnp.concatenate([zero[:3], right], axis=1)
        mid, left, right = high_part(q + half)
        p = q + half + 3
        xs1[p, MARGIN : MARGIN + cols, :] = jnp.concatenate([mid, zero[:cols]], axis=1)
        xs1[p, MARGIN - 3 : MARGIN, :] = jnp.concatenate([left, zero[:3]], axis=1)
        xs1[p, MARGIN + cols : MARGIN + cols + 3, :] = jnp.concatenate([right, zero[:3]], axis=1)

    @pl.loop(0, cols // 8)
    def _(j):
        base = pl.multiple_of(j * 8, 8)
        acc = [None] * rows
        for b in range(7):
            taps = [k0[tap_index(a, b, flipped)] for a in range(7)]
            for r in range(rows):
                x = xs0[r, pl.ds(base + (MARGIN - 3 + b), 8), :]
                for a in range(7):
                    o = r + 3 - a
                    if 0 <= o < rows:
                        term = taps[a] * x
                        acc[o] = term if acc[o] is None else acc[o] + term
        for o in range(rows):
            out_ref[o, pl.ds(base, 8), :128] = acc[o]
        acc = [None] * half
        for b in range(7):
            taps = [k1[tap_index(a, b, flipped)] for a in range(7)]
            for q in range(half + 6):
                x = xs1[q, pl.ds(base + (MARGIN - 3 + b), 8), :]
                for a in range(7):
                    o = q - a
                    if 0 <= o < half:
                        term = taps[a] * x
                        acc[o] = term if acc[o] is None else acc[o] + term
        for o in range(half):
            out_ref[o, pl.ds(base, 8), 128:] = acc[o][:, :64]
            out_ref[o + half, pl.ds(base, 8), 128:] = acc[o][:, 64:]


def conv_scratch(rows, cols):
    return [
        pltpu.VMEM((rows, cols + 2 * MARGIN, 128), F32),
        pltpu.VMEM((rows // 2 + 6, cols + 2 * MARGIN, 128), F32),
        pltpu.VMEM((49, 8, 128), F32),
        pltpu.VMEM((49, 8, 128), F32),
    ]


def conv_kernel(layer, flipped, f_ref, lon_ref, taps_ref, out_ref, *scratch):
    def load_row(r):
        return f_ref[r].astype(BF16).astype(F32)

    conv_local(load_row, lon_ref, taps_ref, layer, out_ref, *scratch, flipped)


def first_conv_kernel(
    area_ref, f_ref, lon_ref, taps_ref, inv_ref, turned_ref, out_ref, sum_ref, inv_out, normed_out, *scratch
):
    rows, cols, _ = f_ref.shape
    start = lax.axis_index("lat") * rows

    def load_row(r):
        return f_ref[r].astype(BF16).astype(F32)

    sum_ref[...] = jnp.zeros_like(sum_ref)

    @pl.loop(0, rows)
    def _(r):
        x = f_ref[r]
        sum_ref[...] += area_ref[0, start + r] * jnp.sum(x * x, axis=0, keepdims=True)

    for layer in range(inv_ref.shape[0]):
        turned = jnp.transpose(inv_ref[layer])
        for r in range(rows):
            inv_out[layer, r] = jnp.broadcast_to(turned[:, r : r + 1], (cols, 128))

        @pl.loop(0, rows)
        def _(r):
            normed_out[layer, r] = jnp.transpose(turned_ref[layer, r].astype(F32)).astype(BF16)

    conv_local(load_row, lon_ref, taps_ref, 0, out_ref, *scratch, False)


def place_halo(parity, a_ref, b_ref, hx):
    cols = a_ref.shape[1] - EXT
    for ref, first in ((a_ref, (1 - parity) * 3), (b_ref, parity * 3)):
        for e in range(3):
            row = ref[e].astype(F32)
            for lanes, plane in ((slice(0, 128), 0), (slice(128, 192), 1)):
                part = row[:, lanes]
                width = part.shape[1]
                hx[plane, first + e, MARGIN : MARGIN + cols, :width] = part[:cols]
                hx[plane, first + e, MARGIN - 3 : MARGIN, :width] = part[cols : cols + 3]
                hx[plane, first + e, MARGIN + cols : MARGIN + cols + 3, :width] = part[cols + 3 : cols + 6]


def conv_halo(hx, acc_ref, taps_ref, layer, edge, k0, k1, flipped):
    rows, cols, _ = acc_ref.shape
    fill_taps(taps_ref, layer, k0, k1)

    @pl.loop(0, cols // 8)
    def _(j):
        base = pl.multiple_of(j * 8, 8)
        for plane, taps_scr, lanes in ((0, k0, slice(0, 128)), (1, k1, slice(128, 192))):
            acc = [None] * 6
            for b in range(7):
                for e in range(3):
                    upper = hx[plane, e, pl.ds(base + (MARGIN - 3 + b), 8), :]
                    for o in range(e + 1):
                        term = taps_scr[tap_index(e - o, b, flipped)] * upper
                        acc[o] = term if acc[o] is None else acc[o] + term
                    lower = hx[plane, 3 + e, pl.ds(base + (MARGIN - 3 + b), 8), :]
                    for p in range(e, 3):
                        term = taps_scr[tap_index(6 + e - p, b, flipped)] * lower
                        acc[3 + p] = term if acc[3 + p] is None else acc[3 + p] + term
            for o in range(6):
                own = o if o < 3 else rows - 6 + o
                width = lanes.stop - lanes.start
                edge[o, pl.ds(base, 8), lanes] = acc_ref[own, pl.ds(base, 8), lanes] + acc[o][:, :width]


def halo_scratch(cols, chans):
    return [
        pltpu.VMEM((2, 6, cols + 2 * MARGIN, 128), F32),
        pltpu.VMEM((6, cols, chans), F32),
        pltpu.VMEM((49, 8, 128), F32),
        pltpu.VMEM((49, 8, 128), F32),
    ]


def wide(inv, chans):
    return jnp.concatenate([inv, inv[:, : chans - 128]], axis=1)


def project(y, normed, inv):
    chans = y.shape[1]
    normal = normed.astype(F32)
    first = jnp.sum(y, axis=1, keepdims=True) * (1.0 / chans)
    second = jnp.sum(normal * y, axis=1, keepdims=True) * (1.0 / chans)
    return wide(inv, chans) * (y - first - normal * second)


ACROSS = (((1,), (1,)), ((), ()))


def forward_net(y, normed, inv, slope, gain, w_in, w_out_turned, scale):
    operand = (gain * project(y, normed, inv)).astype(BF16)
    hidden = jnp.dot(operand, w_in, preferred_element_type=F32)
    gated = (slope.astype(F32) * hidden).astype(BF16)
    return scale * lax.dot_general(gated, w_out_turned, ACROSS, preferred_element_type=F32)


def adjoint_net(g, normed, inv, slope, gain, w_in, w_out_turned, scale):
    scaled = (scale * g).astype(BF16)
    hidden = jnp.dot(scaled, w_out_turned, preferred_element_type=F32)
    gated = (slope.astype(F32) * hidden).astype(BF16)
    back = lax.dot_general(gated, w_in, ACROSS, preferred_element_type=F32)
    return project(gain * back, normed, inv).astype(BF16)


def send_rows(parity, field, lon_ref, a_ref, b_ref):
    rows, cols = lon_ref.shape[0], a_ref.shape[1] - EXT
    for e in range(3):
        top, bottom = field(e), field(rows - 3 + e)
        a_ref[e, :cols, :] = jnp.where(parity == 1, top.astype(F32), bottom.astype(F32)).astype(BF16)
        b_ref[e, :cols, :] = jnp.where(parity == 1, bottom.astype(F32), top.astype(F32)).astype(BF16)
    pad = jnp.zeros((2, lon_ref.shape[2]), BF16)

    @pl.loop(0, rows)
    def _(r):
        row = field(r)
        lon_ref[r] = jnp.concatenate([row[cols - 3 :], row[:3], pad], axis=0)


def flat(x):
    return x.reshape(x.shape[0] * x.shape[1], x.shape[2])


def each_block(rows, fn):
    fn(0, 3, 0)
    fn(rows - 3, 3, 3)

    @pl.loop(0, (rows - 6) // 2)
    def _(i):
        fn(3 + 2 * i, 2, None)


def sums_of(acc_ref, edge, first, count, slot):
    return flat(acc_ref[pl.ds(first, count)]) if slot is None else flat(edge[slot : slot + count])


def net_operands(layer, first, count, refs):
    normed_ref, inv_ref, slope_ref, gain_ref, win_ref, wout_ref, scale_ref = refs
    per_cell = [flat(ref[layer, pl.ds(first, count)]) for ref in (normed_ref, inv_ref, slope_ref)]
    return per_cell + [
        gain_ref[layer : layer + 1, :], win_ref[layer], wout_ref[layer], scale_ref[layer : layer + 1, :]
    ]


def tangent_kernel(layer, last, area_ref, acc_ref, a_ref, b_ref, taps_ref, t_ref, *rest):
    net, rest = rest[:7], rest[7:]
    rows, cols, chans = acc_ref.shape
    lat = lax.axis_index("lat")
    parity = lat % 2
    if last:
        g_ref, db_ref, sum_ref, lon_ref, sa_ref, sb_ref, hx, edge, k0, k1 = rest
        sum_ref[...] = jnp.zeros_like(sum_ref)
    else:
        t_out, lon_ref, sa_ref, sb_ref, hx, edge, k0, k1 = rest
    place_halo(parity, a_ref, b_ref, hx)
    conv_halo(hx, acc_ref, taps_ref, layer, edge, k0, k1, False)

    def block(first, count, slot):
        y = sums_of(acc_ref, edge, first, count, slot)
        operands = net_operands(layer, first, count, net)
        t = flat(t_ref[pl.ds(first, count)]) + forward_net(y, *operands)
        if not last:
            t_out[pl.ds(first, count)] = t.reshape(count, cols, chans)
            return
        parts = []
        for i in range(count):
            u = t[i * cols : (i + 1) * cols]
            g = area_ref[0, lat * rows + first + i] * u
            sum_ref[...] += jnp.sum(g * u, axis=0, keepdims=True)
            parts.append(g)
        g = jnp.concatenate(parts, axis=0)
        g_ref[pl.ds(first, count)] = g.reshape(count, cols, chans)
        db_ref[pl.ds(first, count)] = adjoint_net(g, *operands).reshape(count, cols, chans)

    each_block(rows, block)
    send_rows(parity, (lambda r: db_ref[r]) if last else (lambda r: t_out[r].astype(BF16)), lon_ref, sa_ref, sb_ref)


def adjoint_kernel(layer, acc_ref, a_ref, b_ref, taps_ref, g_ref, *rest):
    net, (g_out, db_ref, lon_ref, sa_ref, sb_ref, hx, edge, k0, k1) = rest[:7], rest[7:]
    rows, cols, chans = acc_ref.shape
    parity = lax.axis_index("lat") % 2
    place_halo(parity, a_ref, b_ref, hx)
    conv_halo(hx, acc_ref, taps_ref, layer + 1, edge, k0, k1, True)

    def block(first, count, slot):
        g = flat(g_ref[pl.ds(first, count)]) + sums_of(acc_ref, edge, first, count, slot)
        g_out[pl.ds(first, count)] = g.reshape(count, cols, chans)
        db = adjoint_net(g, *net_operands(layer, first, count, net))
        db_ref[pl.ds(first, count)] = db.reshape(count, cols, chans)

    each_block(rows, block)
    send_rows(parity, lambda r: db_ref[r], lon_ref, sa_ref, sb_ref)


def final_kernel(
    area_ref, acc_ref, a_ref, b_ref, taps_ref, g_ref, vv_ref, uu_ref, w_ref, tile_ref, hx, edge, k0, k1, ww
):
    rows = acc_ref.shape[0]
    lat = lax.axis_index("lat")
    place_halo(lat % 2, a_ref, b_ref, hx)
    conv_halo(hx, acc_ref, taps_ref, 0, edge, k0, k1, True)
    ww[...] = jnp.zeros_like(ww)

    def row(r, y):
        g = g_ref[r] + y
        w = g * area_ref[1, lat * rows + r]
        w_ref[r] = jnp.transpose(w)
        ww[...] += jnp.sum(g * w, axis=0, keepdims=True)

    for e in range(3):
        row(e, edge[e])
        row(rows - 3 + e, edge[3 + e])

    @pl.loop(3, rows - 3)
    def _(r):
        row(r, acc_ref[r])

    which = lax.broadcasted_iota(jnp.int32, (8, 128), 0)
    vv, uu, wv = (jnp.sum(ref[...]) for ref in (vv_ref, uu_ref, ww))
    tile = jnp.where(which == 0, vv, jnp.where(which == 1, uu, jnp.where(which == 2, wv, 0.0)))
    for i in range(tile_ref.shape[0]):
        tile_ref[i] = tile


def scale_kernel(total, tile_ref, w_ref, out_ref, growth_ref):
    sums = jnp.sum(tile_ref[...], axis=0) * (1.0 / total)
    vv, uu, ww = sums[0:1, :], sums[1:2, :], sums[2:3, :]
    growth_ref[...] = jnp.sqrt(uu / (vv + 1e-06))
    factor = 1.0 / jnp.sqrt(ww + 1e-06)
    i = pl.program_id(0)
    count = out_ref.shape[0]
    for r in range(count):
        out_ref[r] = w_ref[i * count + r] * factor


def extend_kernel(lon_ref, sa_in, sb_in, sa_ref, sb_ref):
    rows, cols = lon_ref.shape[0], sa_ref.shape[1] - EXT
    parity = lax.axis_index("lat") % 2
    for e in range(3):
        sa_ref[e, :cols, :] = sa_in[e, :cols, :]
        sb_ref[e, :cols, :] = sb_in[e, :cols, :]
        sa_ref[e, cols:, :] = lon_ref[(1 - parity) * (rows - 3) + e]
        sb_ref[e, cols:, :] = lon_ref[parity * (rows - 3) + e]


def edges_kernel(turned_ref, t_ref, lon_ref, sa_ref, sb_ref):
    rows = turned_ref.shape[0]

    @pl.loop(0, rows)
    def _(r):
        t_ref[r] = jnp.transpose(turned_ref[r])

    send_rows(lax.axis_index("lat") % 2, lambda r: t_ref[r].astype(BF16), lon_ref, sa_ref, sb_ref)


def params():
    return pltpu.CompilerParams(vmem_limit_bytes=16 * 1024 * 1024)


def on_device(lat_size, lon_size, perturb, kernels, gains, w_in, w_out, scales, normed, inv_std, slope):
    rows, cols, chans = perturb.shape
    hidden = w_in.shape[2]
    layers = kernels.shape[0]
    lat_total = rows * lat_size
    angles = LAT_SPAN * (np.arange(lat_total) + 0.5) / lat_total
    total = float(np.sum(np.cos(angles))) * cols * lon_size * chans
    table = np.stack([np.cos(angles), 1.0 / np.cos(angles)]).astype(np.float32)
    area = jnp.asarray(table)
    across_cells = jnp.transpose(w_out, (0, 2, 1))
    swap_a = [(i, i ^ 1) for i in range(lat_size) if i ^ 1 < lat_size]
    swap_b = [pair for i in range(1, lat_size - 1, 2) for pair in ((i, i + 1), (i + 1, i))]
    swap_lon = [(i, (i + 1) % lon_size) for i in range(lon_size)]

    lon_shape = VMEM((rows, EXT, chans), BF16)
    send_shape = VMEM((3, cols + EXT, chans), BF16)
    full32 = VMEM((rows, cols, chans), F32)
    full16 = VMEM((rows, cols, chans), BF16)
    sums = VMEM((1, chans), F32)

    def call(kernel, out_shape, in_specs, args, scratch=(), flops=0, name=None):
        args = [in_vmem(x) if spec is IN_VMEM else x for spec, x in zip(in_specs, args)]
        return pl.pallas_call(
            kernel,
            out_shape=out_shape,
            in_specs=in_specs,
            out_specs=[IN_VMEM] * len(out_shape),
            scratch_shapes=list(scratch),
            compiler_params=params(),
            cost_estimate=pl.CostEstimate(flops=flops, bytes_accessed=4_000_000, transcendentals=0),
            name=name,
        )(*args)

    def exchange(lon, send_a, send_b):
        side = lax.ppermute(lon, "lon", swap_lon)
        send_a, send_b = call(
            extend_kernel, [send_shape] * 2, [IN_VMEM] * 3, (side, send_a, send_b), name="extend"
        )
        halo_b = lax.ppermute(send_b, "lat", swap_b)
        halo_a = lax.ppermute(send_a, "lat", swap_a)
        return side, halo_a, halo_b

    conv_flops = 2 * 49 * rows * cols * chans
    net_flops = 4 * rows * cols * chans * hidden
    kscr = conv_scratch(rows, cols)
    hscr = halo_scratch(cols, chans)

    tangent, lon, send_a, send_b = call(
        edges_kernel, [full32, lon_shape, send_shape, send_shape], [IN_VMEM], (jnp.transpose(perturb, (0, 2, 1)),),
        name="edges",
    )
    side, halo_a, halo_b = exchange(lon, send_a, send_b)
    acc, vv, inv_wide, normed_cells = call(
        first_conv_kernel,
        [full32, sums, VMEM((layers, rows, cols, 128), F32), VMEM((layers, rows, cols, chans), BF16)],
        [IN_SMEM] + [IN_VMEM] * 5,
        (area, tangent, side, kernels, inv_std, jnp.transpose(normed, (0, 1, 3, 2))), kscr, conv_flops, "conv_first",
    )
    net = (normed_cells, inv_wide, slope, gains, w_in, across_cells, scales)
    for layer in range(layers):
        last = layer == layers - 1
        outs = [full32, full16, sums] if last else [full32]
        outs = outs + [lon_shape, send_shape, send_shape]
        got = call(
            functools.partial(tangent_kernel, layer, last), outs, [IN_SMEM] + [IN_VMEM] * 12,
            (area, acc, halo_a, halo_b, kernels, tangent) + net, hscr, net_flops, f"tangent{layer}",
        )
        side, halo_a, halo_b = exchange(*got[-3:])
        if last:
            grad, back, uu = got[:3]
        else:
            tangent = got[0]
            (acc,) = call(
                functools.partial(conv_kernel, layer + 1, False), [full32], [IN_VMEM] * 3, (tangent, side, kernels),
                kscr, conv_flops, f"conv{layer + 1}",
            )
    for layer in range(layers - 1, -1, -1):
        (acc,) = call(
            functools.partial(conv_kernel, layer, True), [full32], [IN_VMEM] * 3, (back, side, kernels),
            kscr, conv_flops, f"convt{layer}",
        )
        if layer > 0:
            grad, back, lon, send_a, send_b = call(
                functools.partial(adjoint_kernel, layer - 1), [full32, full16, lon_shape, send_shape, send_shape],
                [IN_VMEM] * 12, (acc, halo_a, halo_b, kernels, grad) + net, hscr, net_flops, f"adjoint{layer - 1}",
            )
            side, halo_a, halo_b = exchange(lon, send_a, send_b)
    members = lat_size * lon_size
    w, tile = call(
        final_kernel, [VMEM((rows, chans, cols), F32), VMEM((members, 8, 128), F32)], [IN_SMEM] + [IN_VMEM] * 7,
        (area, acc, halo_a, halo_b, kernels, grad, vv, uu), hscr + [pltpu.VMEM((1, chans), F32)], 0, "final",
    )
    tile = lax.all_to_all(tile, ("lat", "lon"), 0, 0, tiled=True)
    steps = 4
    new_vec, growth = pl.pallas_call(
        functools.partial(scale_kernel, total),
        grid=(steps,),
        out_shape=[jax.ShapeDtypeStruct((rows, chans, cols), F32), jax.ShapeDtypeStruct((1, 128), F32)],
        in_specs=[IN_VMEM, IN_VMEM],
        out_specs=[
            pl.BlockSpec((rows // steps, chans, cols), lambda i: (i, 0, 0)),
            pl.BlockSpec((1, 128), lambda i: (0, 0)),
        ],
        compiler_params=params(),
        name="scale",
    )(in_vmem(tile), in_vmem(w))
    return jnp.transpose(new_vec, (0, 2, 1)), growth[0, :1]


def solution(mesh):
    in_specs = (
        P(("grp", "lat"), "lon", None),
        P(),
        P(),
        P(),
        P(),
        P(),
        P(None, ("grp", "lat"), "lon", None),
        P(None, ("grp", "lat"), "lon"),
        P(None, ("grp", "lat"), "lon", None),
    )
    out_specs = (P(("grp", "lat"), "lon", None), P("grp"))
    fn = functools.partial(on_device, mesh.shape["lat"], mesh.shape["lon"])
    return jax.shard_map(fn, mesh=mesh, in_specs=in_specs, out_specs=out_specs, check_vma=False)
```

```python
import functools
import math

import jax
import jax.numpy as jnp
import numpy as np
from jax import lax
from jax.experimental import pallas as pl
from jax.experimental.pallas import tpu as pltpu
from jax.sharding import PartitionSpec as P

F32 = jnp.float32
BF16 = jnp.bfloat16
LAT_SPAN = 70.0 * math.pi / 180.0
MARGIN = 8
EXT = 16
VMEM = pltpu.VMEM
ACROSS = (((1,), (1,)), ((), ()))
IN_VMEM = pl.BlockSpec(memory_space=pltpu.VMEM)
IN_HBM = pl.BlockSpec(memory_space=pltpu.HBM)
IN_SMEM = pl.BlockSpec(memory_space=pltpu.SMEM)


def in_vmem(x):
    return pltpu.with_memory_space_constraint(x, pltpu.VMEM)


def tap_index(a, b, flipped):
    return (6 - a) * 7 + (6 - b) if flipped else a * 7 + b


def spread_taps(taps_ref, k0, k1, k2):
    for layer in range(taps_ref.shape[0]):
        for a in range(7):
            rows = taps_ref[layer, a]
            for b in range(7):
                row = rows[b : b + 1, :]
                k0[layer, a * 7 + b] = jnp.broadcast_to(row[:, :128], (8, 128))
                high = jnp.broadcast_to(row[:, 128:], (8, row.shape[1] - 128))
                k1[layer, a * 7 + b] = jnp.concatenate([high, high], axis=1)
        lane = lax.broadcasted_iota(jnp.int32, (8, 128), 1)
        for a in range(3):
            for b in range(7):
                for flipped in (0, 1):
                    low = k1[layer, tap_index(a, b, flipped)]
                    high = k1[layer, tap_index(6 - a, b, flipped)]
                    k2[layer, flipped, a * 7 + b] = jnp.where(lane < 64, low, high)


def fill_row(xs, index, mid, side):
    cols = mid.shape[0]
    xs[index, :MARGIN, :] = side[:MARGIN]
    xs[index, MARGIN : MARGIN + cols, :] = mid
    xs[index, MARGIN + cols :, :] = side[MARGIN:]


def conv_local(load_row, lon_ref, k0, k1, layer, out_ref, xs0, xs1, flipped, beside=None):
    rows, cols, _ = out_ref.shape
    half = rows // 2

    @pl.loop(0, half)
    def _(r):
        low, high = load_row(r), load_row(r + half)
        low_side, high_side = lon_ref[r].astype(F32), lon_ref[r + half].astype(F32)
        fill_row(xs0, r, low[:, :128], low_side[:, :128])
        fill_row(xs0, r + half, high[:, :128], high_side[:, :128])
        mid = jnp.concatenate([low[:, 128:], high[:, 128:]], axis=1)
        side = jnp.concatenate([low_side[:, 128:], high_side[:, 128:]], axis=1)
        fill_row(xs1, r + 3, mid, side)

    lane = lax.broadcasted_iota(jnp.int32, (cols + 2 * MARGIN, 128), 1)
    for q in range(3):
        above, below = xs1[q + half], xs1[q + 3]
        xs1[q] = jnp.where(lane < 64, 0.0, pltpu.roll(above, 64, 1))
        xs1[q + half + 3] = jnp.where(lane < 64, pltpu.roll(below, 64, 1), 0.0)

    @pl.loop(0, cols // 8)
    def _(j):
        base = pl.multiple_of(j * 8, 8)
        acc = [None] * rows
        for b in range(7):
            taps = [k0[layer, tap_index(a, b, flipped)] for a in range(7)]
            for r in range(rows):
                x = xs0[r, pl.ds(base + (MARGIN - 3 + b), 8), :]
                for a in range(7):
                    o = r + 3 - a
                    if 0 <= o < rows:
                        term = taps[a] * x
                        acc[o] = term if acc[o] is None else acc[o] + term
        for o in range(rows):
            out_ref[o, pl.ds(base, 8), :128] = acc[o]
        acc = [None] * half
        for b in range(7):
            taps = [k1[layer, tap_index(a, b, flipped)] for a in range(7)]
            for q in range(half + 6):
                x = xs1[q, pl.ds(base + (MARGIN - 3 + b), 8), :]
                for a in range(7):
                    o = q - a
                    if 0 <= o < half:
                        term = taps[a] * x
                        acc[o] = term if acc[o] is None else acc[o] + term
        for o in range(half):
            out_ref[o, pl.ds(base, 8), 128:] = acc[o][:, :64]
            out_ref[o + half, pl.ds(base, 8), 128:] = acc[o][:, 64:]
        if beside is not None:
            beside(j)


def conv_scratch(rows, cols):
    return [
        pltpu.VMEM((rows, cols + 2 * MARGIN, 128), F32),
        pltpu.VMEM((rows // 2 + 6, cols + 2 * MARGIN, 128), F32),
    ]


def conv_kernel(layer, flipped, f_ref, lon_ref, k0, k1, out_ref, *scratch):
    def load_row(r):
        return f_ref[r].astype(BF16).astype(F32)

    conv_local(load_row, lon_ref, k0, k1, layer, out_ref, *scratch, flipped)


def first_conv_kernel(
    area_ref, f_ref, lon_ref, taps_ref, inv_ref, turned_ref, slope_hbm, out_ref, sum_ref, inv_out, normed_out,
    k0, k1, k2, slope_out, xs0, xs1, sems,
):
    rows, cols, _ = f_ref.shape
    start = lax.axis_index("lat") * rows
    fetches = [
        pltpu.make_async_copy(slope_hbm.at[layer], slope_out.at[layer], sems.at[layer])
        for layer in range(slope_hbm.shape[0])
    ]
    for fetch in fetches:
        fetch.start()
    spread_taps(taps_ref, k0, k1, k2)
    one = lax.broadcasted_iota(jnp.int32, (cols, cols), 0) == lax.broadcasted_iota(jnp.int32, (cols, cols), 1)
    eye = jnp.where(one, 1.0, 0.0).astype(BF16)

    def turn_row(r):
        x = f_ref[r]
        sum_ref[...] += area_ref[0, start + r] * jnp.sum(x * x, axis=0, keepdims=True)
        for layer in range(inv_ref.shape[0]):
            turned = lax.dot_general(eye, turned_ref[layer, r], ACROSS, preferred_element_type=F32)
            normed_out[layer, r] = turned.astype(BF16)
            inv = inv_ref[layer, pl.ds(r, 1), :]
            inv_out[layer, r] = jnp.transpose(jnp.broadcast_to(inv, (128, cols)))

    def load_row(r):
        return f_ref[r].astype(BF16).astype(F32)

    sum_ref[...] = jnp.zeros_like(sum_ref)
    steps = cols // 8
    for j in range(steps, rows):
        turn_row(j)

    def beside(j):
        if rows >= steps:
            turn_row(j)
        else:
            pl.when(j < rows)(lambda: turn_row(j))

    conv_local(load_row, lon_ref, k0, k1, 0, out_ref, xs0, xs1, False, beside)
    for fetch in fetches:
        fetch.wait()


def place_halo(parity, a_ref, b_ref, h0, h1):
    cols = a_ref.shape[1] - EXT

    def put(ref, index, row):
        ref[index, :MARGIN, :] = row[cols : cols + MARGIN]
        ref[index, MARGIN : MARGIN + cols, :] = row[:cols]
        ref[index, MARGIN + cols :, :] = row[cols + MARGIN :]

    for e in range(3):
        put(h0, (1 - parity) * 3 + e, a_ref[e, :, :128].astype(F32))
        put(h0, parity * 3 + e, b_ref[e, :, :128].astype(F32))
        a_up, a_down = a_ref[e, :, 128:].astype(F32), a_ref[2 - e, :, 128:].astype(F32)
        b_up, b_down = b_ref[e, :, 128:].astype(F32), b_ref[2 - e, :, 128:].astype(F32)
        up, down = jnp.where(parity == 1, a_up, b_up), jnp.where(parity == 1, b_down, a_down)
        put(h1, e, jnp.concatenate([up, down], axis=1))


def conv_halo(h0, h1, acc_ref, k0, k2, layer, edge, flipped):
    rows, cols, _ = acc_ref.shape
    unroll = 2

    def add(acc, index, term):
        acc[index] = term if acc[index] is None else acc[index] + term

    @pl.loop(0, cols // (8 * unroll))
    def _(block):
        bases = [pl.multiple_of(block * (8 * unroll) + 8 * i, 8) for i in range(unroll)]
        acc = [[None] * 6 for _ in bases]
        for b in range(7):
            taps = {a: k0[layer, tap_index(a, b, flipped)] for a in (0, 1, 2, 4, 5, 6)}
            for i, base in enumerate(bases):
                for e in range(3):
                    upper = h0[e, pl.ds(base + (MARGIN - 3 + b), 8), :]
                    for o in range(e + 1):
                        add(acc[i], o, taps[e - o] * upper)
                    lower = h0[3 + e, pl.ds(base + (MARGIN - 3 + b), 8), :]
                    for p in range(e, 3):
                        add(acc[i], 3 + p, taps[6 + e - p] * lower)
        for i, base in enumerate(bases):
            for o in range(6):
                own = o if o < 3 else rows - 6 + o
                edge[o, pl.ds(base, 8), :128] = acc_ref[own, pl.ds(base, 8), :128] + acc[i][o]
        acc = [[None] * 3 for _ in bases]
        for b in range(7):
            taps = [k2[layer, int(flipped), a * 7 + b] for a in range(3)]
            for i, base in enumerate(bases):
                for e in range(3):
                    both = h1[e, pl.ds(base + (MARGIN - 3 + b), 8), :]
                    for o in range(e + 1):
                        add(acc[i], o, taps[e - o] * both)
        for i, base in enumerate(bases):
            for o in range(3):
                edge[o, pl.ds(base, 8), 128:] = acc_ref[o, pl.ds(base, 8), 128:] + acc[i][o][:, :64]
                own = acc_ref[rows - 1 - o, pl.ds(base, 8), 128:]
                edge[5 - o, pl.ds(base, 8), 128:] = own + acc[i][o][:, 64:]


def halo_scratch(cols, chans):
    return [
        pltpu.VMEM((6, cols + 2 * MARGIN, 128), F32),
        pltpu.VMEM((3, cols + 2 * MARGIN, 128), F32),
        pltpu.VMEM((6, cols, chans), F32),
    ]


def wide(inv, chans):
    return jnp.concatenate([inv, inv[:, : chans - 128]], axis=1)


def project(y, normed, inv):
    chans = y.shape[1]
    normal = normed.astype(F32)
    first = jnp.sum(y, axis=1, keepdims=True) * (1.0 / chans)
    second = jnp.sum(normal * y, axis=1, keepdims=True) * (1.0 / chans)
    return inv * (y - first - normal * second)


def forward_net(y, normed, inv, slope, gain, w_in, w_out_turned, scale):
    operand = (gain * project(y, normed, inv)).astype(BF16)
    hidden = jnp.dot(operand, w_in, preferred_element_type=F32)
    gated = (slope.astype(F32) * hidden).astype(BF16)
    return scale * lax.dot_general(gated, w_out_turned, ACROSS, preferred_element_type=F32)


def adjoint_net(g, normed, inv, slope, gain, w_in, w_out_turned, scale):
    scaled = (scale * g).astype(BF16)
    hidden = jnp.dot(scaled, w_out_turned, preferred_element_type=F32)
    gated = (slope.astype(F32) * hidden).astype(BF16)
    back = lax.dot_general(gated, w_in, ACROSS, preferred_element_type=F32)
    return project(gain * back, normed, inv).astype(BF16)


def send_rows(parity, field, lon_ref, a_ref, b_ref):
    rows, cols = field.shape[0], field.shape[1]
    for e in range(3):
        a_ref[e, :cols, :] = field[(1 - parity) * (rows - 3) + e].astype(BF16)
        b_ref[e, :cols, :] = field[parity * (rows - 3) + e].astype(BF16)
    for r in range(rows):
        lon_ref[r, :MARGIN, :] = field[r, cols - MARGIN :, :].astype(BF16)
        lon_ref[r, MARGIN:, :] = field[r, :MARGIN, :].astype(BF16)


def flat(x):
    return x.reshape(x.shape[0] * x.shape[1], x.shape[2])


class Rows:
    def __init__(self, rows, outer):
        self.spans = [(0, 3), (rows - 3, 3)] if outer else [(3, rows - 6)]

    def get(self, ref, *lead):
        return jnp.concatenate([flat(ref[(*lead, slice(a, a + n))]) for a, n in self.spans], axis=0)

    def put(self, ref, value):
        cols, done = ref.shape[1], 0
        for a, n in self.spans:
            ref[a : a + n] = value[done * cols : (done + n) * cols].reshape(n, cols, value.shape[1])
            done += n

    def numbers(self):
        return [a + i for a, n in self.spans for i in range(n)]


def both_blocks(acc_ref, edge, fn):
    rows = acc_ref.shape[0]
    inner, outer = Rows(rows, False), Rows(rows, True)
    fn(outer, flat(edge[...]))
    fn(inner, inner.get(acc_ref))


def net_operands(layer, block, refs):
    normed_ref, inv_ref, slope_ref, gain_ref, win_ref, wout_ref, scale_ref = refs
    return [
        block.get(normed_ref, layer), wide(block.get(inv_ref, layer), normed_ref.shape[3]), block.get(slope_ref, layer),
        gain_ref[layer : layer + 1, :], win_ref[layer], wout_ref[layer], scale_ref[layer : layer + 1, :],
    ]


def tangent_kernel(layer, last, area_ref, acc_ref, a_ref, b_ref, k0, k2, t_ref, *rest):
    net, rest = rest[:7], rest[7:]
    rows, cols, chans = acc_ref.shape
    lat = lax.axis_index("lat")
    if last:
        g_ref, db_ref, sum_ref, lon_ref, sa_ref, sb_ref, h0, h1, edge = rest
        sum_ref[...] = jnp.zeros_like(sum_ref)
    else:
        t_out, lon_ref, sa_ref, sb_ref, h0, h1, edge = rest
    place_halo(lat % 2, a_ref, b_ref, h0, h1)
    conv_halo(h0, h1, acc_ref, k0, k2, layer, edge, False)

    def work(block, y):
        operands = net_operands(layer, block, net)
        t = block.get(t_ref) + forward_net(y, *operands)
        if not last:
            block.put(t_out, t)
            return
        parts = []
        for i, r in enumerate(block.numbers()):
            u = t[i * cols : (i + 1) * cols]
            g = area_ref[0, lat * rows + r] * u
            sum_ref[...] += jnp.sum(g * u, axis=0, keepdims=True)
            parts.append(g)
        g = jnp.concatenate(parts, axis=0)
        block.put(g_ref, g)
        block.put(db_ref, adjoint_net(g, *operands))

    both_blocks(acc_ref, edge, work)
    send_rows(lat % 2, db_ref if last else t_out, lon_ref, sa_ref, sb_ref)


def adjoint_kernel(layer, acc_ref, a_ref, b_ref, k0, k2, g_ref, *rest):
    net, (g_out, db_ref, lon_ref, sa_ref, sb_ref, h0, h1, edge) = rest[:7], rest[7:]
    parity = lax.axis_index("lat") % 2
    place_halo(parity, a_ref, b_ref, h0, h1)
    conv_halo(h0, h1, acc_ref, k0, k2, layer + 1, edge, True)

    def work(block, y):
        g = block.get(g_ref) + y
        block.put(g_out, g)
        block.put(db_ref, adjoint_net(g, *net_operands(layer, block, net)))

    both_blocks(acc_ref, edge, work)
    send_rows(parity, db_ref, lon_ref, sa_ref, sb_ref)


def final_kernel(
    area_ref, acc_ref, a_ref, b_ref, k0, k2, g_ref, vv_ref, uu_ref, w_ref, tile_ref, h0, h1, edge, ww
):
    rows = acc_ref.shape[0]
    lat = lax.axis_index("lat")
    place_halo(lat % 2, a_ref, b_ref, h0, h1)
    conv_halo(h0, h1, acc_ref, k0, k2, 0, edge, True)
    ww[...] = jnp.zeros_like(ww)

    def row(r, y):
        g = g_ref[r] + y
        w = g * area_ref[1, lat * rows + r]
        w_ref[r] = jnp.transpose(w)
        ww[...] += jnp.sum(g * w, axis=0, keepdims=True)

    for e in range(3):
        row(e, edge[e])
        row(rows - 3 + e, edge[3 + e])

    for r in range(3, rows - 3):
        row(r, acc_ref[r])

    which = lax.broadcasted_iota(jnp.int32, (8, 128), 0)
    vv, uu, wv = (jnp.sum(ref[...]) for ref in (vv_ref, uu_ref, ww))
    tile = jnp.where(which == 0, vv, jnp.where(which == 1, uu, jnp.where(which == 2, wv, 0.0)))
    for i in range(tile_ref.shape[0]):
        tile_ref[i] = tile


def scale_kernel(total, tile_ref, w_ref, out_hbm, growth_ref, scaled, sems):
    sums = jnp.sum(tile_ref[...], axis=0) * (1.0 / total)
    vv, uu, ww = sums[0:1, :], sums[1:2, :], sums[2:3, :]
    growth_ref[...] = jnp.sqrt(uu / (vv + 1e-06))
    factor = 1.0 / jnp.sqrt(ww + 1e-06)
    copies = []
    for r in range(w_ref.shape[0]):
        scaled[r] = w_ref[r] * factor
        copies.append(pltpu.make_async_copy(scaled.at[r], out_hbm.at[r], sems.at[r]))
        copies[-1].start()
    for copy in copies:
        copy.wait()


def extend_kernel(lon_ref, sa_in, sb_in, sa_ref, sb_ref):
    rows, cols = lon_ref.shape[0], sa_ref.shape[1] - EXT
    parity = lax.axis_index("lat") % 2
    for e in range(3):
        sa_ref[e, :cols, :] = sa_in[e, :cols, :]
        sb_ref[e, :cols, :] = sb_in[e, :cols, :]
        sa_ref[e, cols:, :] = lon_ref[(1 - parity) * (rows - 3) + e]
        sb_ref[e, cols:, :] = lon_ref[parity * (rows - 3) + e]


def edges_kernel(turned_hbm, t_ref, lon_ref, sa_ref, sb_ref, turned, sems):
    rows = turned.shape[0]
    copies = [pltpu.make_async_copy(turned_hbm.at[r], turned.at[r], sems.at[r]) for r in range(rows)]
    for copy in copies:
        copy.start()
    for r, copy in enumerate(copies):
        copy.wait()
        t_ref[r] = jnp.transpose(turned[r])
    send_rows(lax.axis_index("lat") % 2, t_ref, lon_ref, sa_ref, sb_ref)


def params():
    return pltpu.CompilerParams(vmem_limit_bytes=16 * 1024 * 1024)


def on_device(lat_size, lon_size, perturb, kernels, gains, w_in, w_out, scales, normed, inv_std, slope):
    rows, cols, chans = perturb.shape
    hidden = w_in.shape[2]
    layers = kernels.shape[0]
    lat_total = rows * lat_size
    angles = LAT_SPAN * (np.arange(lat_total) + 0.5) / lat_total
    total = float(np.sum(np.cos(angles))) * cols * lon_size * chans
    table = np.stack([np.cos(angles), 1.0 / np.cos(angles)]).astype(np.float32)
    area = jnp.asarray(table)
    across_cells = jnp.transpose(w_out, (0, 2, 1))
    swap_a = [(i, i ^ 1) for i in range(lat_size) if i ^ 1 < lat_size]
    swap_b = [pair for i in range(1, lat_size - 1, 2) for pair in ((i, i + 1), (i + 1, i))]
    swap_lon = [(i, (i + 1) % lon_size) for i in range(lon_size)]

    lon_shape = VMEM((rows, EXT, chans), BF16)
    send_shape = VMEM((3, cols + EXT, chans), BF16)
    full32 = VMEM((rows, cols, chans), F32)
    full16 = VMEM((rows, cols, chans), BF16)
    sums = VMEM((1, chans), F32)

    def call(kernel, out_shape, in_specs, args, scratch=(), flops=0, name=None):
        args = [pltpu.with_memory_space_constraint(x, spec.memory_space) if spec is not IN_SMEM else x for spec, x in zip(in_specs, args)]
        return pl.pallas_call(
            kernel,
            out_shape=out_shape,
            in_specs=in_specs,
            out_specs=[IN_VMEM] * len(out_shape),
            scratch_shapes=list(scratch),
            compiler_params=params(),
            cost_estimate=pl.CostEstimate(flops=flops, bytes_accessed=4_000_000, transcendentals=0),
            name=name,
        )(*args)

    def exchange(lon, send_a, send_b):
        side = lax.ppermute(lon, "lon", swap_lon)
        send_a, send_b = call(
            extend_kernel, [send_shape] * 2, [IN_VMEM] * 3, (side, send_a, send_b), name="extend"
        )
        halo_a = lax.ppermute(send_a, "lat", swap_a)
        halo_b = lax.ppermute(send_b, "lat", swap_b)
        return side, halo_a, halo_b

    conv_flops = 2 * 49 * rows * cols * chans
    net_flops = 4 * rows * cols * chans * hidden
    kscr = conv_scratch(rows, cols)
    hscr = halo_scratch(cols, chans)

    tangent, lon, send_a, send_b = call(
        edges_kernel, [full32, lon_shape, send_shape, send_shape], [IN_HBM], (jnp.transpose(perturb, (0, 2, 1)),),
        [pltpu.VMEM((rows, chans, cols), F32), pltpu.SemaphoreType.DMA((rows,))], name="edges",
    )
    side, halo_a, halo_b = exchange(lon, send_a, send_b)
    acc, vv, inv_cells, normed_cells, k0, k1, k2, slope_cells = call(
        first_conv_kernel,
        [
            full32, sums, VMEM((layers, rows, cols, 128), F32), VMEM((layers, rows, cols, chans), BF16),
            VMEM((layers, 49, 8, 128), F32), VMEM((layers, 49, 8, 128), F32), VMEM((layers, 2, 21, 8, 128), F32),
            VMEM(slope.shape, BF16),
        ],
        [IN_SMEM] + [IN_VMEM] * 5 + [IN_HBM],
        (area, tangent, side, kernels, inv_std, jnp.transpose(normed, (0, 1, 3, 2)), slope),
        kscr + [pltpu.SemaphoreType.DMA((layers,))], conv_flops, "conv_first",
    )
    net = (normed_cells, inv_cells, slope_cells, gains, w_in, across_cells, scales)
    for layer in range(layers):
        last = layer == layers - 1
        outs = [full32, full16, sums] if last else [full32]
        outs = outs + [lon_shape, send_shape, send_shape]
        got = call(
            functools.partial(tangent_kernel, layer, last), outs, [IN_SMEM] + [IN_VMEM] * 13,
            (area, acc, halo_a, halo_b, k0, k2, tangent) + net, hscr, net_flops, f"tangent{layer}",
        )
        side, halo_a, halo_b = exchange(*got[-3:])
        if last:
            grad, back, uu = got[:3]
        else:
            tangent = got[0]
            (acc,) = call(
                functools.partial(conv_kernel, layer + 1, False), [full32], [IN_VMEM] * 4, (tangent, side, k0, k1),
                kscr, conv_flops, f"conv{layer + 1}",
            )
    for layer in range(layers - 1, -1, -1):
        (acc,) = call(
            functools.partial(conv_kernel, layer, True), [full32], [IN_VMEM] * 4, (back, side, k0, k1),
            kscr, conv_flops, f"convt{layer}",
        )
        if layer > 0:
            grad, back, lon, send_a, send_b = call(
                functools.partial(adjoint_kernel, layer - 1), [full32, full16, lon_shape, send_shape, send_shape],
                [IN_VMEM] * 13, (acc, halo_a, halo_b, k0, k2, grad) + net, hscr, net_flops, f"adjoint{layer - 1}",
            )
            side, halo_a, halo_b = exchange(lon, send_a, send_b)
    members = lat_size * lon_size
    w, tile = call(
        final_kernel, [VMEM((rows, chans, cols), F32), VMEM((members, 8, 128), F32)], [IN_SMEM] + [IN_VMEM] * 8,
        (area, acc, halo_a, halo_b, k0, k2, grad, vv, uu), hscr + [pltpu.VMEM((1, chans), F32)], 0, "final",
    )
    tile = lax.all_to_all(tile, ("lat", "lon"), 0, 0, tiled=True)
    new_vec, growth = pl.pallas_call(
        functools.partial(scale_kernel, total),
        out_shape=[jax.ShapeDtypeStruct((rows, chans, cols), F32), jax.ShapeDtypeStruct((1, 128), F32)],
        in_specs=[IN_VMEM, IN_VMEM],
        out_specs=[IN_HBM, IN_VMEM],
        scratch_shapes=[pltpu.VMEM((rows, chans, cols), F32), pltpu.SemaphoreType.DMA((rows,))],
        compiler_params=params(),
        name="scale",
    )(in_vmem(tile), in_vmem(w))
    return jnp.transpose(new_vec, (0, 2, 1)), growth[0, :1]


def solution(mesh):
    in_specs = (
        P(("grp", "lat"), "lon", None),
        P(),
        P(),
        P(),
        P(),
        P(),
        P(None, ("grp", "lat"), "lon", None),
        P(None, ("grp", "lat"), "lon"),
        P(None, ("grp", "lat"), "lon", None),
    )
    out_specs = (P(("grp", "lat"), "lon", None), P("grp"))
    fn = functools.partial(on_device, mesh.shape["lat"], mesh.shape["lon"])
    return jax.shard_map(fn, mesh=mesh, in_specs=in_specs, out_specs=out_specs, check_vma=False)
```

```python
import functools
import math

import jax
import jax.numpy as jnp
import numpy as np
from jax import lax
from jax.experimental import pallas as pl
from jax.experimental.pallas import tpu as pltpu
from jax.sharding import PartitionSpec as P

F32 = jnp.float32
BF16 = jnp.bfloat16
LAT_SPAN = 70.0 * math.pi / 180.0
MARGIN = 8
EXT = 16
VMEM = pltpu.VMEM
ACROSS = (((1,), (1,)), ((), ()))
IN_VMEM = pl.BlockSpec(memory_space=pltpu.VMEM)
IN_HBM = pl.BlockSpec(memory_space=pltpu.HBM)
IN_SMEM = pl.BlockSpec(memory_space=pltpu.SMEM)


def in_vmem(x):
    return pltpu.with_memory_space_constraint(x, pltpu.VMEM)


def tap_index(a, b, flipped):
    return (6 - a) * 7 + (6 - b) if flipped else a * 7 + b


def spread_taps(taps_ref, k0, k1):
    for layer in range(taps_ref.shape[2]):

        def low(index):
            return jnp.broadcast_to(taps_ref[index // 7, index % 7, layer : layer + 1, :128], (8, 128))

        def high(index):
            row = taps_ref[index // 7, index % 7, layer : layer + 1, 128:]
            return jnp.broadcast_to(row, (8, row.shape[1]))

        for a in range(7):
            for b in range(7):
                k0[layer, a * 7 + b] = low(a * 7 + b)
                for flipped in (0, 1):
                    pair = [high(tap_index(a, b, flipped)), high(tap_index(6 - a, b, flipped))]
                    k1[layer, flipped, a * 7 + b] = jnp.concatenate(pair, axis=1)


def fill_row(xs, index, mid, side):
    cols = mid.shape[0]
    xs[index, :MARGIN, :] = side[:MARGIN]
    xs[index, MARGIN : MARGIN + cols, :] = mid
    xs[index, MARGIN + cols :, :] = side[MARGIN:]


def conv_local(load_row, lon_ref, k0, k1, layer, out_ref, xs0, xs1, flipped, beside=None):
    rows, cols, _ = out_ref.shape
    half = rows // 2

    def fill(q, wide_too):
        low, high = load_row(q), load_row(rows - 1 - q)
        low_side, high_side = lon_ref[q].astype(F32), lon_ref[rows - 1 - q].astype(F32)
        if wide_too:
            fill_row(xs0, q, low[:, :128], low_side[:, :128])
            fill_row(xs0, rows - 1 - q, high[:, :128], high_side[:, :128])
        mid = jnp.concatenate([low[:, 128:], high[:, 128:]], axis=1)
        side = jnp.concatenate([low_side[:, 128:], high_side[:, 128:]], axis=1)
        fill_row(xs1, q, mid, side)

    @pl.loop(0, half)
    def _(q):
        fill(q, True)

    for q in range(half, half + 3):
        fill(q, False)

    @pl.loop(0, cols // 8)
    def _(j):
        base = pl.multiple_of(j * 8, 8)
        acc = [None] * rows
        for b in range(7):
            taps = [k0[layer, tap_index(a, b, flipped)] for a in range(7)]
            for r in range(rows):
                x = xs0[r, pl.ds(base + (MARGIN - 3 + b), 8), :]
                for a in range(7):
                    o = r + 3 - a
                    if 0 <= o < rows:
                        term = taps[a] * x
                        acc[o] = term if acc[o] is None else acc[o] + term
        for o in range(rows):
            out_ref[o, pl.ds(base, 8), :128] = acc[o]
        acc = [None] * half
        for b in range(7):
            taps = [k1[layer, int(flipped), a * 7 + b] for a in range(7)]
            for q in range(half + 3):
                x = xs1[q, pl.ds(base + (MARGIN - 3 + b), 8), :]
                for a in range(7):
                    o = q + 3 - a
                    if 0 <= o < half:
                        term = taps[a] * x
                        acc[o] = term if acc[o] is None else acc[o] + term
        for o in range(half):
            out_ref[o, pl.ds(base, 8), 128:] = acc[o][:, :64]
            out_ref[rows - 1 - o, pl.ds(base, 8), 128:] = acc[o][:, 64:]
        if beside is not None:
            beside(j)


def conv_scratch(rows, cols):
    return [
        pltpu.VMEM((rows, cols + 2 * MARGIN, 128), F32),
        pltpu.VMEM((rows // 2 + 3, cols + 2 * MARGIN, 128), F32),
    ]


def conv_kernel(layer, flipped, f_ref, lon_ref, k0, k1, out_ref, *scratch):
    def load_row(r):
        return f_ref[r].astype(BF16).astype(F32)

    conv_local(load_row, lon_ref, k0, k1, layer, out_ref, *scratch, flipped)


def first_conv_kernel(
    area_ref, f_ref, lon_ref, k0, k1, turned_ref, slope_hbm, out_ref, sum_ref, normed_out, slope_out, xs0, xs1, sems
):
    rows, cols, _ = f_ref.shape
    start = lax.axis_index("lat") * rows
    fetches = [
        pltpu.make_async_copy(slope_hbm.at[layer], slope_out.at[layer], sems.at[layer])
        for layer in range(slope_hbm.shape[0])
    ]
    for fetch in fetches:
        fetch.start()
    one = lax.broadcasted_iota(jnp.int32, (cols, cols), 0) == lax.broadcasted_iota(jnp.int32, (cols, cols), 1)
    eye = jnp.where(one, 1.0, 0.0).astype(BF16)

    def turn_row(r):
        x = f_ref[r]
        sum_ref[...] += area_ref[0, start + r] * jnp.sum(x * x, axis=0, keepdims=True)
        for layer in range(turned_ref.shape[0]):
            turned = lax.dot_general(eye, turned_ref[layer, r], ACROSS, preferred_element_type=F32)
            normed_out[layer, r] = turned.astype(BF16)

    def load_row(r):
        return f_ref[r].astype(BF16).astype(F32)

    sum_ref[...] = jnp.zeros_like(sum_ref)
    steps = cols // 8
    for j in range(steps, rows):
        turn_row(j)

    def beside(j):
        if rows >= steps:
            turn_row(j)
        else:
            pl.when(j < rows)(lambda: turn_row(j))

    conv_local(load_row, lon_ref, k0, k1, 0, out_ref, xs0, xs1, False, beside)
    for fetch in fetches:
        fetch.wait()


def place_halo(parity, a_ref, b_ref, h0, h1):
    cols = a_ref.shape[1] - EXT

    def put(ref, index, row):
        ref[index, :MARGIN, :] = row[cols : cols + MARGIN]
        ref[index, MARGIN : MARGIN + cols, :] = row[:cols]
        ref[index, MARGIN + cols :, :] = row[cols + MARGIN :]

    for e in range(3):
        put(h0, (1 - parity) * 3 + e, a_ref[e, :, :128].astype(F32))
        put(h0, parity * 3 + e, b_ref[e, :, :128].astype(F32))
        a_up, a_down = a_ref[e, :, 128:].astype(F32), a_ref[2 - e, :, 128:].astype(F32)
        b_up, b_down = b_ref[e, :, 128:].astype(F32), b_ref[2 - e, :, 128:].astype(F32)
        up, down = jnp.where(parity == 1, a_up, b_up), jnp.where(parity == 1, b_down, a_down)
        put(h1, e, jnp.concatenate([up, down], axis=1))


def conv_halo(h0, h1, acc_ref, k0, k1, layer, edge, flipped):
    rows, cols, _ = acc_ref.shape
    unroll = 2

    def add(acc, index, term):
        acc[index] = term if acc[index] is None else acc[index] + term

    @pl.loop(0, cols // (8 * unroll))
    def _(block):
        bases = [pl.multiple_of(block * (8 * unroll) + 8 * i, 8) for i in range(unroll)]
        acc = [[None] * 6 for _ in bases]
        for b in range(7):
            taps = {a: k0[layer, tap_index(a, b, flipped)] for a in (0, 1, 2, 4, 5, 6)}
            for i, base in enumerate(bases):
                for e in range(3):
                    upper = h0[e, pl.ds(base + (MARGIN - 3 + b), 8), :]
                    for o in range(e + 1):
                        add(acc[i], o, taps[e - o] * upper)
                    lower = h0[3 + e, pl.ds(base + (MARGIN - 3 + b), 8), :]
                    for p in range(e, 3):
                        add(acc[i], 3 + p, taps[6 + e - p] * lower)
        for i, base in enumerate(bases):
            for o in range(6):
                own = o if o < 3 else rows - 6 + o
                edge[o, pl.ds(base, 8), :128] = acc_ref[own, pl.ds(base, 8), :128] + acc[i][o]
        acc = [[None] * 3 for _ in bases]
        for b in range(7):
            taps = [k1[layer, int(flipped), a * 7 + b] for a in range(3)]
            for i, base in enumerate(bases):
                for e in range(3):
                    both = h1[e, pl.ds(base + (MARGIN - 3 + b), 8), :]
                    for o in range(e + 1):
                        add(acc[i], o, taps[e - o] * both)
        for i, base in enumerate(bases):
            for o in range(3):
                edge[o, pl.ds(base, 8), 128:] = acc_ref[o, pl.ds(base, 8), 128:] + acc[i][o][:, :64]
                own = acc_ref[rows - 1 - o, pl.ds(base, 8), 128:]
                edge[5 - o, pl.ds(base, 8), 128:] = own + acc[i][o][:, 64:]


def halo_scratch(cols, chans):
    return [
        pltpu.VMEM((6, cols + 2 * MARGIN, 128), F32),
        pltpu.VMEM((3, cols + 2 * MARGIN, 128), F32),
        pltpu.VMEM((6, cols, chans), F32),
    ]


def wide(inv, chans):
    return jnp.concatenate([inv, inv[:, : chans - 128]], axis=1)


def project(y, normed, inv):
    chans = y.shape[1]
    normal = normed.astype(F32)
    first = jnp.sum(y, axis=1, keepdims=True) * (1.0 / chans)
    second = jnp.sum(normal * y, axis=1, keepdims=True) * (1.0 / chans)
    return inv * (y - first - normal * second)


def forward_net(y, normed, inv, slope, gain, w_in, w_out_turned, scale):
    operand = (gain * project(y, normed, inv)).astype(BF16)
    hidden = jnp.dot(operand, w_in, preferred_element_type=F32)
    gated = (slope.astype(F32) * hidden).astype(BF16)
    return scale * lax.dot_general(gated, w_out_turned, ACROSS, preferred_element_type=F32)


def adjoint_net(g, normed, inv, slope, gain, w_in, w_out_turned, scale):
    scaled = (scale * g).astype(BF16)
    hidden = jnp.dot(scaled, w_out_turned, preferred_element_type=F32)
    gated = (slope.astype(F32) * hidden).astype(BF16)
    back = lax.dot_general(gated, w_in, ACROSS, preferred_element_type=F32)
    return project(gain * back, normed, inv).astype(BF16)


def send_rows(parity, field, lon_ref, a_ref, b_ref):
    rows, cols = field.shape[0], field.shape[1]
    for e in range(3):
        a_ref[e, :cols, :] = field[(1 - parity) * (rows - 3) + e].astype(BF16)
        b_ref[e, :cols, :] = field[parity * (rows - 3) + e].astype(BF16)
    for r in range(rows):
        lon_ref[r, :MARGIN, :] = field[r, cols - MARGIN :, :].astype(BF16)
        lon_ref[r, MARGIN:, :] = field[r, :MARGIN, :].astype(BF16)


def flat(x):
    return x.reshape(x.shape[0] * x.shape[1], x.shape[2])


class Rows:
    def __init__(self, rows, outer):
        self.spans = [(0, 3), (rows - 3, 3)] if outer else [(3, rows - 6)]

    def get(self, ref, *lead):
        return jnp.concatenate([flat(ref[(*lead, slice(a, a + n))]) for a, n in self.spans], axis=0)

    def put(self, ref, value):
        cols, done = ref.shape[1], 0
        for a, n in self.spans:
            ref[a : a + n] = value[done * cols : (done + n) * cols].reshape(n, cols, value.shape[1])
            done += n

    def numbers(self):
        return [a + i for a, n in self.spans for i in range(n)]


def both_blocks(acc_ref, edge, fn):
    rows = acc_ref.shape[0]
    inner, outer = Rows(rows, False), Rows(rows, True)
    fn(outer, flat(edge[...]))
    fn(inner, inner.get(acc_ref))


def net_operands(layer, block, refs):
    normed_ref, inv_ref, slope_ref, gain_ref, win_ref, wout_ref, scale_ref = refs
    return [
        block.get(normed_ref, layer), wide(block.get(inv_ref, layer), normed_ref.shape[3]), block.get(slope_ref, layer),
        gain_ref[layer : layer + 1, :], win_ref[layer], wout_ref[layer], scale_ref[layer : layer + 1, :],
    ]


def tangent_kernel(layer, last, area_ref, acc_ref, a_ref, b_ref, k0, k1, t_ref, *rest):
    net, rest = rest[:7], rest[7:]
    rows, cols, chans = acc_ref.shape
    lat = lax.axis_index("lat")
    if last:
        g_ref, db_ref, sum_ref, lon_ref, sa_ref, sb_ref, h0, h1, edge = rest
        sum_ref[...] = jnp.zeros_like(sum_ref)
    else:
        t_out, lon_ref, sa_ref, sb_ref, h0, h1, edge = rest
    place_halo(lat % 2, a_ref, b_ref, h0, h1)
    conv_halo(h0, h1, acc_ref, k0, k1, layer, edge, False)

    def work(block, y):
        operands = net_operands(layer, block, net)
        t = block.get(t_ref) + forward_net(y, *operands)
        if not last:
            block.put(t_out, t)
            return
        parts = []
        for i, r in enumerate(block.numbers()):
            u = t[i * cols : (i + 1) * cols]
            g = area_ref[0, lat * rows + r] * u
            sum_ref[...] += jnp.sum(g * u, axis=0, keepdims=True)
            parts.append(g)
        g = jnp.concatenate(parts, axis=0)
        block.put(g_ref, g)
        block.put(db_ref, adjoint_net(g, *operands))

    both_blocks(acc_ref, edge, work)
    send_rows(lat % 2, db_ref if last else t_out, lon_ref, sa_ref, sb_ref)


def adjoint_kernel(layer, acc_ref, a_ref, b_ref, k0, k1, g_ref, *rest):
    net, (g_out, db_ref, lon_ref, sa_ref, sb_ref, h0, h1, edge) = rest[:7], rest[7:]
    parity = lax.axis_index("lat") % 2
    place_halo(parity, a_ref, b_ref, h0, h1)
    conv_halo(h0, h1, acc_ref, k0, k1, layer + 1, edge, True)

    def work(block, y):
        g = block.get(g_ref) + y
        block.put(g_out, g)
        block.put(db_ref, adjoint_net(g, *net_operands(layer, block, net)))

    both_blocks(acc_ref, edge, work)
    send_rows(parity, db_ref, lon_ref, sa_ref, sb_ref)


def final_kernel(
    area_ref, acc_ref, a_ref, b_ref, k0, k1, g_ref, vv_ref, uu_ref, w_ref, tile_ref, h0, h1, edge, ww
):
    rows = acc_ref.shape[0]
    lat = lax.axis_index("lat")
    place_halo(lat % 2, a_ref, b_ref, h0, h1)
    conv_halo(h0, h1, acc_ref, k0, k1, 0, edge, True)
    ww[...] = jnp.zeros_like(ww)

    def row(r, y):
        g = g_ref[r] + y
        w = g * area_ref[1, lat * rows + r]
        w_ref[r] = jnp.transpose(w)
        ww[...] += jnp.sum(g * w, axis=0, keepdims=True)

    for e in range(3):
        row(e, edge[e])
        row(rows - 3 + e, edge[3 + e])

    for r in range(3, rows - 3):
        row(r, acc_ref[r])

    which = lax.broadcasted_iota(jnp.int32, (1, 128), 1)
    vv, uu, wv = (jnp.sum(ref[...]) for ref in (vv_ref, uu_ref, ww))
    tile = jnp.where(which == 0, vv, jnp.where(which == 1, uu, jnp.where(which == 2, wv, 0.0)))
    for i in range(tile_ref.shape[0]):
        tile_ref[i] = tile


def scale_kernel(total, tile_ref, w_ref, out_hbm, growth_ref, scaled, sems):
    sums = jnp.sum(tile_ref[...], axis=0) * (1.0 / total)
    vv, uu, ww = (jnp.broadcast_to(sums[:, i : i + 1], (1, 128)) for i in range(3))
    growth_ref[...] = jnp.sqrt(uu / (vv + 1e-06))
    factor = 1.0 / jnp.sqrt(ww + 1e-06)
    copies = []
    for r in range(w_ref.shape[0]):
        scaled[r] = w_ref[r] * factor
        copies.append(pltpu.make_async_copy(scaled.at[r], out_hbm.at[r], sems.at[r]))
        copies[-1].start()
    for copy in copies:
        copy.wait()


def extend_kernel(lon_ref, sa_in, sb_in, sa_ref, sb_ref):
    rows, cols = lon_ref.shape[0], sa_ref.shape[1] - EXT
    parity = lax.axis_index("lat") % 2
    for e in range(3):
        sa_ref[e, :cols, :] = sa_in[e, :cols, :]
        sb_ref[e, :cols, :] = sb_in[e, :cols, :]
        sa_ref[e, cols:, :] = lon_ref[(1 - parity) * (rows - 3) + e]
        sb_ref[e, cols:, :] = lon_ref[parity * (rows - 3) + e]


def edges_kernel(
    turned_hbm, taps_hbm, inv_hbm, t_ref, lon_ref, sa_ref, sb_ref, k0, k1, inv_out, turned, taps_ref, inv_ref, sems
):
    rows = turned.shape[0]
    copies = [pltpu.make_async_copy(turned_hbm.at[r], turned.at[r], sems.at[r]) for r in range(rows)]
    small = [
        pltpu.make_async_copy(inv_hbm, inv_ref, sems.at[rows]),
        pltpu.make_async_copy(taps_hbm, taps_ref, sems.at[rows + 1]),
    ]
    for copy in small + copies:
        copy.start()
    for copy in small:
        copy.wait()
    spread_taps(taps_ref, k0, k1)
    for layer in range(inv_ref.shape[0]):
        for r in range(rows):
            inv = jnp.broadcast_to(inv_ref[layer, r : r + 1, :], (128, inv_ref.shape[2]))
            inv_out[layer, r] = jnp.transpose(inv)
    for r, copy in enumerate(copies):
        copy.wait()
        t_ref[r] = jnp.transpose(turned[r])
    send_rows(lax.axis_index("lat") % 2, t_ref, lon_ref, sa_ref, sb_ref)


def params():
    return pltpu.CompilerParams(vmem_limit_bytes=16 * 1024 * 1024)


def on_device(lat_size, lon_size, perturb, kernels, gains, w_in, w_out, scales, normed, inv_std, slope):
    rows, cols, chans = perturb.shape
    hidden = w_in.shape[2]
    layers = kernels.shape[0]
    lat_total = rows * lat_size
    angles = LAT_SPAN * (np.arange(lat_total) + 0.5) / lat_total
    total = float(np.sum(np.cos(angles))) * cols * lon_size * chans
    table = np.stack([np.cos(angles), 1.0 / np.cos(angles)]).astype(np.float32)
    area = jnp.asarray(table)
    across_cells = jnp.transpose(w_out, (0, 2, 1))
    swap_a = [(i, i ^ 1) for i in range(lat_size) if i ^ 1 < lat_size]
    swap_b = [pair for i in range(1, lat_size - 1, 2) for pair in ((i, i + 1), (i + 1, i))]
    swap_lon = [(i, (i + 1) % lon_size) for i in range(lon_size)]

    lon_shape = VMEM((rows, EXT, chans), BF16)
    send_shape = VMEM((3, cols + EXT, chans), BF16)
    full32 = VMEM((rows, cols, chans), F32)
    full16 = VMEM((rows, cols, chans), BF16)
    sums = VMEM((1, chans), F32)

    def call(kernel, out_shape, in_specs, args, scratch=(), flops=0, name=None):
        args = [pltpu.with_memory_space_constraint(x, spec.memory_space) if spec is not IN_SMEM else x for spec, x in zip(in_specs, args)]
        return pl.pallas_call(
            kernel,
            out_shape=out_shape,
            in_specs=in_specs,
            out_specs=[IN_VMEM] * len(out_shape),
            scratch_shapes=list(scratch),
            compiler_params=params(),
            cost_estimate=pl.CostEstimate(flops=flops, bytes_accessed=4_000_000, transcendentals=0),
            name=name,
        )(*args)

    def exchange(lon, send_a, send_b):
        side = lax.ppermute(lon, "lon", swap_lon)
        send_a, send_b = call(
            extend_kernel, [send_shape] * 2, [IN_VMEM] * 3, (side, send_a, send_b), name="extend"
        )
        halo_a = lax.ppermute(send_a, "lat", swap_a)
        halo_b = lax.ppermute(send_b, "lat", swap_b)
        return side, halo_a, halo_b

    conv_flops = 2 * 49 * rows * cols * chans
    net_flops = 4 * rows * cols * chans * hidden
    kscr = conv_scratch(rows, cols)
    hscr = halo_scratch(cols, chans)

    tangent, lon, send_a, send_b, k0, k1, inv_cells = call(
        edges_kernel,
        [
            full32, lon_shape, send_shape, send_shape, VMEM((layers, 49, 8, 128), F32),
            VMEM((layers, 2, 49, 8, 128), F32), VMEM((layers, rows, cols, 128), F32),
        ],
        [IN_HBM] * 3, (jnp.transpose(perturb, (0, 2, 1)), jnp.transpose(kernels, (1, 2, 0, 3)), inv_std),
        [
            pltpu.VMEM((rows, chans, cols), F32), pltpu.VMEM((7, 7, layers, chans), F32),
            pltpu.VMEM(inv_std.shape, F32), pltpu.SemaphoreType.DMA((rows + 2,)),
        ],
        name="edges",
    )
    side, halo_a, halo_b = exchange(lon, send_a, send_b)
    acc, vv, normed_cells, slope_cells = call(
        first_conv_kernel,
        [full32, sums, VMEM((layers, rows, cols, chans), BF16), VMEM(slope.shape, BF16)],
        [IN_SMEM] + [IN_VMEM] * 5 + [IN_HBM],
        (area, tangent, side, k0, k1, jnp.transpose(normed, (0, 1, 3, 2)), slope),
        kscr + [pltpu.SemaphoreType.DMA((layers,))], conv_flops, "conv_first",
    )
    net = (normed_cells, inv_cells, slope_cells, gains, w_in, across_cells, scales)
    for layer in range(layers):
        last = layer == layers - 1
        outs = [full32, full16, sums] if last else [full32]
        outs = outs + [lon_shape, send_shape, send_shape]
        got = call(
            functools.partial(tangent_kernel, layer, last), outs, [IN_SMEM] + [IN_VMEM] * 13,
            (area, acc, halo_a, halo_b, k0, k1, tangent) + net, hscr, net_flops, f"tangent{layer}",
        )
        side, halo_a, halo_b = exchange(*got[-3:])
        if last:
            grad, back, uu = got[:3]
        else:
            tangent = got[0]
            (acc,) = call(
                functools.partial(conv_kernel, layer + 1, False), [full32], [IN_VMEM] * 4, (tangent, side, k0, k1),
                kscr, conv_flops, f"conv{layer + 1}",
            )
    for layer in range(layers - 1, -1, -1):
        (acc,) = call(
            functools.partial(conv_kernel, layer, True), [full32], [IN_VMEM] * 4, (back, side, k0, k1),
            kscr, conv_flops, f"convt{layer}",
        )
        if layer > 0:
            grad, back, lon, send_a, send_b = call(
                functools.partial(adjoint_kernel, layer - 1), [full32, full16, lon_shape, send_shape, send_shape],
                [IN_VMEM] * 13, (acc, halo_a, halo_b, k0, k1, grad) + net, hscr, net_flops, f"adjoint{layer - 1}",
            )
            side, halo_a, halo_b = exchange(lon, send_a, send_b)
    members = lat_size * lon_size
    w, tile = call(
        final_kernel, [VMEM((rows, chans, cols), F32), VMEM((members, 1, 128), F32)], [IN_SMEM] + [IN_VMEM] * 8,
        (area, acc, halo_a, halo_b, k0, k1, grad, vv, uu), hscr + [pltpu.VMEM((1, chans), F32)], 0, "final",
    )
    tile = lax.all_to_all(tile, ("lat", "lon"), 0, 0, tiled=True)
    new_vec, growth = pl.pallas_call(
        functools.partial(scale_kernel, total),
        out_shape=[jax.ShapeDtypeStruct((rows, chans, cols), F32), jax.ShapeDtypeStruct((1, 128), F32)],
        in_specs=[IN_VMEM, IN_VMEM],
        out_specs=[IN_HBM, IN_VMEM],
        scratch_shapes=[pltpu.VMEM((rows, chans, cols), F32), pltpu.SemaphoreType.DMA((rows,))],
        compiler_params=params(),
        name="scale",
    )(in_vmem(tile), in_vmem(w))
    return jnp.transpose(new_vec, (0, 2, 1)), growth[0, :1]


def solution(mesh):
    in_specs = (
        P(("grp", "lat"), "lon", None),
        P(),
        P(),
        P(),
        P(),
        P(),
        P(None, ("grp", "lat"), "lon", None),
        P(None, ("grp", "lat"), "lon"),
        P(None, ("grp", "lat"), "lon", None),
    )
    out_specs = (P(("grp", "lat"), "lon", None), P("grp"))
    fn = functools.partial(on_device, mesh.shape["lat"], mesh.shape["lon"])
    return jax.shard_map(fn, mesh=mesh, in_specs=in_specs, out_specs=out_specs, check_vma=False)
```

```python
import functools
import math

import jax
import jax.numpy as jnp
import numpy as np
from jax import lax
from jax.experimental import pallas as pl
from jax.experimental.pallas import tpu as pltpu
from jax.sharding import PartitionSpec as P

F32 = jnp.float32
BF16 = jnp.bfloat16
LAT_SPAN = 70.0 * math.pi / 180.0
MARGIN = 8
EXT = 16
VMEM = pltpu.VMEM
ACROSS = (((1,), (1,)), ((), ()))
IN_VMEM = pl.BlockSpec(memory_space=pltpu.VMEM)
IN_HBM = pl.BlockSpec(memory_space=pltpu.HBM)
IN_SMEM = pl.BlockSpec(memory_space=pltpu.SMEM)


def in_vmem(x):
    return pltpu.with_memory_space_constraint(x, pltpu.VMEM)


def tap_index(a, b, flipped):
    return (6 - a) * 7 + (6 - b) if flipped else a * 7 + b


def spread_taps(taps_ref, k0, k1):
    for layer in range(taps_ref.shape[2]):

        def low(index):
            return jnp.broadcast_to(taps_ref[index // 7, index % 7, layer : layer + 1, :128], (8, 128))

        def high(index):
            row = taps_ref[index // 7, index % 7, layer : layer + 1, 128:]
            return jnp.broadcast_to(row, (8, row.shape[1]))

        for a in range(7):
            for b in range(7):
                k0[layer, a * 7 + b] = low(a * 7 + b)
                for flipped in (0, 1):
                    pair = [high(tap_index(a, b, flipped)), high(tap_index(6 - a, b, flipped))]
                    k1[layer, flipped, a * 7 + b] = jnp.concatenate(pair, axis=1)


def fill_row(xs, index, mid, side):
    cols = mid.shape[0]
    xs[index, :MARGIN, :] = side[:MARGIN]
    xs[index, MARGIN : MARGIN + cols, :] = mid
    xs[index, MARGIN + cols :, :] = side[MARGIN:]


def conv_local(load_row, lon_ref, k0, k1, layer, out_ref, xs0, xs1, flipped, beside=None):
    rows, cols, _ = out_ref.shape
    half = rows // 2

    def fill(q, wide_too):
        low, high = load_row(q), load_row(rows - 1 - q)
        low_side, high_side = lon_ref[q].astype(F32), lon_ref[rows - 1 - q].astype(F32)
        if wide_too:
            fill_row(xs0, q, low[:, :128], low_side[:, :128])
            fill_row(xs0, rows - 1 - q, high[:, :128], high_side[:, :128])
        mid = jnp.concatenate([low[:, 128:], high[:, 128:]], axis=1)
        side = jnp.concatenate([low_side[:, 128:], high_side[:, 128:]], axis=1)
        fill_row(xs1, q, mid, side)

    @pl.loop(0, half)
    def _(q):
        fill(q, True)

    for q in range(half, half + 3):
        fill(q, False)

    @pl.loop(0, cols // 8)
    def _(j):
        base = pl.multiple_of(j * 8, 8)
        acc = [None] * rows
        for b in range(7):
            taps = [k0[layer, tap_index(a, b, flipped)] for a in range(7)]
            for r in range(rows):
                x = xs0[r, pl.ds(base + (MARGIN - 3 + b), 8), :]
                for a in range(7):
                    o = r + 3 - a
                    if 0 <= o < rows:
                        term = taps[a] * x
                        acc[o] = term if acc[o] is None else acc[o] + term
        for o in range(rows):
            out_ref[o, pl.ds(base, 8), :128] = acc[o]
        acc = [None] * half
        for b in range(7):
            taps = [k1[layer, int(flipped), a * 7 + b] for a in range(7)]
            for q in range(half + 3):
                x = xs1[q, pl.ds(base + (MARGIN - 3 + b), 8), :]
                for a in range(7):
                    o = q + 3 - a
                    if 0 <= o < half:
                        term = taps[a] * x
                        acc[o] = term if acc[o] is None else acc[o] + term
        for o in range(half):
            out_ref[o, pl.ds(base, 8), 128:] = acc[o][:, :64]
            out_ref[rows - 1 - o, pl.ds(base, 8), 128:] = acc[o][:, 64:]
        if beside is not None:
            beside(j)


def conv_scratch(rows, cols):
    return [
        pltpu.VMEM((rows, cols + 2 * MARGIN, 128), F32),
        pltpu.VMEM((rows // 2 + 3, cols + 2 * MARGIN, 128), F32),
    ]


def conv_kernel(layer, flipped, f_ref, lon_ref, k0, k1, out_ref, *scratch):
    def load_row(r):
        return f_ref[r].astype(BF16).astype(F32)

    conv_local(load_row, lon_ref, k0, k1, layer, out_ref, *scratch, flipped)


def first_conv_kernel(
    area_ref, f_ref, lon_ref, k0, k1, turned_ref, slope_hbm, out_ref, sum_ref, normed_out, slope_out, xs0, xs1, sems
):
    rows, cols, _ = f_ref.shape
    start = lax.axis_index("lat") * rows
    fetches = [
        pltpu.make_async_copy(slope_hbm.at[layer], slope_out.at[layer], sems.at[layer])
        for layer in range(slope_hbm.shape[0])
    ]
    for fetch in fetches:
        fetch.start()
    one = lax.broadcasted_iota(jnp.int32, (cols, cols), 0) == lax.broadcasted_iota(jnp.int32, (cols, cols), 1)
    eye = jnp.where(one, 1.0, 0.0).astype(BF16)

    def turn_row(r):
        x = f_ref[r]
        sum_ref[...] += area_ref[0, start + r] * jnp.sum(x * x, axis=0, keepdims=True)
        for layer in range(turned_ref.shape[0]):
            turned = lax.dot_general(eye, turned_ref[layer, r], ACROSS, preferred_element_type=F32)
            normed_out[layer, r] = turned.astype(BF16)

    def load_row(r):
        return f_ref[r].astype(BF16).astype(F32)

    sum_ref[...] = jnp.zeros_like(sum_ref)
    steps = cols // 8
    for j in range(steps, rows):
        turn_row(j)

    def beside(j):
        if rows >= steps:
            turn_row(j)
        else:
            pl.when(j < rows)(lambda: turn_row(j))

    conv_local(load_row, lon_ref, k0, k1, 0, out_ref, xs0, xs1, False, beside)
    for fetch in fetches:
        fetch.wait()


def place_halo(parity, a_ref, b_ref, h0, h1):
    width = h0.shape[1]
    cols = width - EXT
    middle = cols // 2
    lane = lax.broadcasted_iota(jnp.int32, (width // 2, 128), 1)
    for e in range(3):
        for ref, first in ((a_ref, (1 - parity) * 3), (b_ref, parity * 3)):
            row = ref[e, :width, :].astype(F32)
            h0[first + e, :MARGIN, :] = row[cols : cols + MARGIN]
            h0[first + e, MARGIN : MARGIN + cols, :] = row[:cols]
            h0[first + e, MARGIN + cols :, :] = row[cols + MARGIN :]
        a_up, a_down = a_ref[e, width:, :].astype(F32), a_ref[2 - e, width:, :].astype(F32)
        b_up, b_down = b_ref[e, width:, :].astype(F32), b_ref[2 - e, width:, :].astype(F32)
        up, down = jnp.where(parity == 1, a_up, b_up), jnp.where(parity == 1, b_down, a_down)
        first = jnp.where(lane < 64, up, pltpu.roll(down, 64, 1))
        second = jnp.where(lane < 64, pltpu.roll(up, 64, 1), down)
        h1[e, :MARGIN, :] = first[middle:]
        h1[e, MARGIN : MARGIN + middle, :] = first[:middle]
        h1[e, MARGIN + middle : MARGIN + cols, :] = second[:middle]
        h1[e, MARGIN + cols :, :] = second[middle:]


def conv_halo(h0, h1, acc_ref, k0, k1, layer, edge, flipped):
    rows, cols, _ = acc_ref.shape
    unroll = 2

    def add(acc, index, term):
        acc[index] = term if acc[index] is None else acc[index] + term

    @pl.loop(0, cols // (8 * unroll))
    def _(block):
        bases = [pl.multiple_of(block * (8 * unroll) + 8 * i, 8) for i in range(unroll)]
        acc = [[None] * 6 for _ in bases]
        for b in range(7):
            taps = {a: k0[layer, tap_index(a, b, flipped)] for a in (0, 1, 2, 4, 5, 6)}
            for i, base in enumerate(bases):
                for e in range(3):
                    upper = h0[e, pl.ds(base + (MARGIN - 3 + b), 8), :]
                    for o in range(e + 1):
                        add(acc[i], o, taps[e - o] * upper)
                    lower = h0[3 + e, pl.ds(base + (MARGIN - 3 + b), 8), :]
                    for p in range(e, 3):
                        add(acc[i], 3 + p, taps[6 + e - p] * lower)
        for i, base in enumerate(bases):
            for o in range(6):
                own = o if o < 3 else rows - 6 + o
                edge[o, pl.ds(base, 8), :128] = acc_ref[own, pl.ds(base, 8), :128] + acc[i][o]
        acc = [[None] * 3 for _ in bases]
        for b in range(7):
            taps = [k1[layer, int(flipped), a * 7 + b] for a in range(3)]
            for i, base in enumerate(bases):
                for e in range(3):
                    both = h1[e, pl.ds(base + (MARGIN - 3 + b), 8), :]
                    for o in range(e + 1):
                        add(acc[i], o, taps[e - o] * both)
        for i, base in enumerate(bases):
            for o in range(3):
                edge[o, pl.ds(base, 8), 128:] = acc_ref[o, pl.ds(base, 8), 128:] + acc[i][o][:, :64]
                own = acc_ref[rows - 1 - o, pl.ds(base, 8), 128:]
                edge[5 - o, pl.ds(base, 8), 128:] = own + acc[i][o][:, 64:]


def halo_scratch(cols, chans):
    return [
        pltpu.VMEM((6, cols + 2 * MARGIN, 128), F32),
        pltpu.VMEM((3, cols + 2 * MARGIN, 128), F32),
        pltpu.VMEM((6, cols, chans), F32),
    ]


def wide(inv, chans):
    return jnp.concatenate([inv, inv[:, : chans - 128]], axis=1)


def project(y, normed, inv):
    chans = y.shape[1]
    normal = normed.astype(F32)
    first = jnp.sum(y, axis=1, keepdims=True) * (1.0 / chans)
    second = jnp.sum(normal * y, axis=1, keepdims=True) * (1.0 / chans)
    return inv * (y - first - normal * second)


def forward_net(y, normed, inv, slope, gain, w_in, w_out_turned, scale):
    operand = (gain * project(y, normed, inv)).astype(BF16)
    hidden = jnp.dot(operand, w_in, preferred_element_type=F32)
    gated = (slope.astype(F32) * hidden).astype(BF16)
    return scale * lax.dot_general(gated, w_out_turned, ACROSS, preferred_element_type=F32)


def adjoint_net(g, normed, inv, slope, gain, w_in, w_out_turned, scale):
    scaled = (scale * g).astype(BF16)
    hidden = jnp.dot(scaled, w_out_turned, preferred_element_type=F32)
    gated = (slope.astype(F32) * hidden).astype(BF16)
    back = lax.dot_general(gated, w_in, ACROSS, preferred_element_type=F32)
    return project(gain * back, normed, inv).astype(BF16)


def fold(values):
    count = values.shape[0] // 2
    return jnp.concatenate([values[:count], values[count:]], axis=1)


def send_rows(parity, field, lon_ref, a_ref, b_ref):
    rows, cols = field.shape[0], field.shape[1]
    width = cols + EXT
    for e in range(3):
        for ref, row in ((a_ref, (1 - parity) * (rows - 3) + e), (b_ref, parity * (rows - 3) + e)):
            ref[e, :cols, :] = field[row, :, :128].astype(BF16)
            ref[e, width : width + cols // 2, :] = fold(field[row, :, 128:].astype(F32)).astype(BF16)
    for r in range(rows):
        lon_ref[r, :MARGIN, :] = field[r, cols - MARGIN :, :].astype(BF16)
        lon_ref[r, MARGIN:, :] = field[r, :MARGIN, :].astype(BF16)


def flat(x):
    return x.reshape(x.shape[0] * x.shape[1], x.shape[2])


class Rows:
    def __init__(self, rows, outer):
        self.spans = [(0, 3), (rows - 3, 3)] if outer else [(3, rows - 6)]

    def get(self, ref, *lead):
        return jnp.concatenate([flat(ref[(*lead, slice(a, a + n))]) for a, n in self.spans], axis=0)

    def put(self, ref, value):
        cols, done = ref.shape[1], 0
        for a, n in self.spans:
            ref[a : a + n] = value[done * cols : (done + n) * cols].reshape(n, cols, value.shape[1])
            done += n

    def numbers(self):
        return [a + i for a, n in self.spans for i in range(n)]


def both_blocks(acc_ref, edge, fn):
    rows = acc_ref.shape[0]
    inner, outer = Rows(rows, False), Rows(rows, True)
    fn(outer, flat(edge[...]))
    fn(inner, inner.get(acc_ref))


def net_operands(layer, block, refs):
    normed_ref, inv_ref, slope_ref, gain_ref, win_ref, wout_ref, scale_ref = refs
    return [
        block.get(normed_ref, layer), wide(block.get(inv_ref, layer), normed_ref.shape[3]), block.get(slope_ref, layer),
        gain_ref[layer : layer + 1, :], win_ref[layer], wout_ref[layer], scale_ref[layer : layer + 1, :],
    ]


def tangent_kernel(layer, last, area_ref, acc_ref, a_ref, b_ref, k0, k1, t_ref, *rest):
    net, rest = rest[:7], rest[7:]
    rows, cols, chans = acc_ref.shape
    lat = lax.axis_index("lat")
    if last:
        g_ref, db_ref, sum_ref, lon_ref, sa_ref, sb_ref, h0, h1, edge = rest
        sum_ref[...] = jnp.zeros_like(sum_ref)
    else:
        t_out, lon_ref, sa_ref, sb_ref, h0, h1, edge = rest
    place_halo(lat % 2, a_ref, b_ref, h0, h1)
    conv_halo(h0, h1, acc_ref, k0, k1, layer, edge, False)

    def work(block, y):
        operands = net_operands(layer, block, net)
        t = block.get(t_ref) + forward_net(y, *operands)
        if not last:
            block.put(t_out, t)
            return
        parts = []
        for i, r in enumerate(block.numbers()):
            u = t[i * cols : (i + 1) * cols]
            g = area_ref[0, lat * rows + r] * u
            sum_ref[...] += jnp.sum(g * u, axis=0, keepdims=True)
            parts.append(g)
        g = jnp.concatenate(parts, axis=0)
        block.put(g_ref, g)
        block.put(db_ref, adjoint_net(g, *operands))

    both_blocks(acc_ref, edge, work)
    send_rows(lat % 2, db_ref if last else t_out, lon_ref, sa_ref, sb_ref)


def adjoint_kernel(layer, acc_ref, a_ref, b_ref, k0, k1, g_ref, *rest):
    net, (g_out, db_ref, lon_ref, sa_ref, sb_ref, h0, h1, edge) = rest[:7], rest[7:]
    parity = lax.axis_index("lat") % 2
    place_halo(parity, a_ref, b_ref, h0, h1)
    conv_halo(h0, h1, acc_ref, k0, k1, layer + 1, edge, True)

    def work(block, y):
        g = block.get(g_ref) + y
        block.put(g_out, g)
        block.put(db_ref, adjoint_net(g, *net_operands(layer, block, net)))

    both_blocks(acc_ref, edge, work)
    send_rows(parity, db_ref, lon_ref, sa_ref, sb_ref)


def final_kernel(
    area_ref, acc_ref, a_ref, b_ref, k0, k1, g_ref, vv_ref, uu_ref, w_ref, tile_ref, h0, h1, edge, ww
):
    rows = acc_ref.shape[0]
    lat = lax.axis_index("lat")
    place_halo(lat % 2, a_ref, b_ref, h0, h1)
    conv_halo(h0, h1, acc_ref, k0, k1, 0, edge, True)
    ww[...] = jnp.zeros_like(ww)

    def row(r, y):
        g = g_ref[r] + y
        w = g * area_ref[1, lat * rows + r]
        w_ref[r] = jnp.transpose(w)
        ww[...] += jnp.sum(g * w, axis=0, keepdims=True)

    for e in range(3):
        row(e, edge[e])
        row(rows - 3 + e, edge[3 + e])

    for r in range(3, rows - 3):
        row(r, acc_ref[r])

    which = lax.broadcasted_iota(jnp.int32, (1, 128), 1)
    vv, uu, wv = (jnp.sum(ref[...]) for ref in (vv_ref, uu_ref, ww))
    tile = jnp.where(which == 0, vv, jnp.where(which == 1, uu, jnp.where(which == 2, wv, 0.0)))
    for i in range(tile_ref.shape[0]):
        tile_ref[i] = tile


def scale_kernel(total, tile_ref, w_ref, out_hbm, growth_ref, scaled, sems):
    sums = jnp.sum(tile_ref[...], axis=0) * (1.0 / total)
    vv, uu, ww = (jnp.broadcast_to(sums[:, i : i + 1], (1, 128)) for i in range(3))
    growth_ref[...] = jnp.sqrt(uu / (vv + 1e-06))
    factor = 1.0 / jnp.sqrt(ww + 1e-06)
    copies = []
    for r in range(w_ref.shape[0]):
        scaled[r] = w_ref[r] * factor
        copies.append(pltpu.make_async_copy(scaled.at[r], out_hbm.at[r], sems.at[r]))
        copies[-1].start()
    for copy in copies:
        copy.wait()


def extend_kernel(lon_ref, sa_in, sb_in, sa_ref, sb_ref):
    rows, width = lon_ref.shape[0], sa_ref.shape[1] // 3 * 2
    cols = width - EXT
    parity = lax.axis_index("lat") % 2
    for e in range(3):
        for source, ref, row in (
            (sa_in, sa_ref, (1 - parity) * (rows - 3) + e), (sb_in, sb_ref, parity * (rows - 3) + e)
        ):
            ref[e, :cols, :] = source[e, :cols, :]
            ref[e, width : width + cols // 2, :] = source[e, width : width + cols // 2, :]
            side = lon_ref[row]
            ref[e, cols:width, :] = side[:, :128]
            ref[e, width + cols // 2 :, :] = fold(side[:, 128:].astype(F32)).astype(BF16)


def edges_kernel(
    turned_hbm, taps_hbm, inv_hbm, t_ref, lon_ref, sa_ref, sb_ref, k0, k1, inv_out, turned, taps_ref, inv_ref, sems
):
    rows = turned.shape[0]
    copies = [pltpu.make_async_copy(turned_hbm.at[r], turned.at[r], sems.at[r]) for r in range(rows)]
    small = [
        pltpu.make_async_copy(inv_hbm, inv_ref, sems.at[rows]),
        pltpu.make_async_copy(taps_hbm, taps_ref, sems.at[rows + 1]),
    ]
    for copy in small + copies:
        copy.start()
    for copy in small:
        copy.wait()
    spread_taps(taps_ref, k0, k1)
    for layer in range(inv_ref.shape[0]):
        for r in range(rows):
            inv = jnp.broadcast_to(inv_ref[layer, r : r + 1, :], (128, inv_ref.shape[2]))
            inv_out[layer, r] = jnp.transpose(inv)
    for r, copy in enumerate(copies):
        copy.wait()
        t_ref[r] = jnp.transpose(turned[r])
    send_rows(lax.axis_index("lat") % 2, t_ref, lon_ref, sa_ref, sb_ref)


def params():
    return pltpu.CompilerParams(vmem_limit_bytes=16 * 1024 * 1024)


def on_device(lat_size, lon_size, perturb, kernels, gains, w_in, w_out, scales, normed, inv_std, slope):
    rows, cols, chans = perturb.shape
    hidden = w_in.shape[2]
    layers = kernels.shape[0]
    lat_total = rows * lat_size
    angles = LAT_SPAN * (np.arange(lat_total) + 0.5) / lat_total
    total = float(np.sum(np.cos(angles))) * cols * lon_size * chans
    table = np.stack([np.cos(angles), 1.0 / np.cos(angles)]).astype(np.float32)
    area = jnp.asarray(table)
    across_cells = jnp.transpose(w_out, (0, 2, 1))
    swap_a = [(i, i ^ 1) for i in range(lat_size) if i ^ 1 < lat_size]
    swap_b = [pair for i in range(1, lat_size - 1, 2) for pair in ((i, i + 1), (i + 1, i))]
    swap_lon = [(i, (i + 1) % lon_size) for i in range(lon_size)]

    lon_shape = VMEM((rows, EXT, chans), BF16)
    send_shape = VMEM((3, (cols + EXT) // 2 * 3, 128), BF16)
    full32 = VMEM((rows, cols, chans), F32)
    full16 = VMEM((rows, cols, chans), BF16)
    sums = VMEM((1, chans), F32)

    def call(kernel, out_shape, in_specs, args, scratch=(), flops=0, name=None):
        args = [pltpu.with_memory_space_constraint(x, spec.memory_space) if spec is not IN_SMEM else x for spec, x in zip(in_specs, args)]
        return pl.pallas_call(
            kernel,
            out_shape=out_shape,
            in_specs=in_specs,
            out_specs=[IN_VMEM] * len(out_shape),
            scratch_shapes=list(scratch),
            compiler_params=params(),
            cost_estimate=pl.CostEstimate(flops=flops, bytes_accessed=4_000_000, transcendentals=0),
            name=name,
        )(*args)

    def exchange(lon, send_a, send_b):
        side = lax.ppermute(lon, "lon", swap_lon)
        send_a, send_b = call(
            extend_kernel, [send_shape] * 2, [IN_VMEM] * 3, (side, send_a, send_b), name="extend"
        )
        halo_a = lax.ppermute(send_a, "lat", swap_a)
        halo_b = lax.ppermute(send_b, "lat", swap_b)
        return side, halo_a, halo_b

    conv_flops = 2 * 49 * rows * cols * chans
    net_flops = 4 * rows * cols * chans * hidden
    kscr = conv_scratch(rows, cols)
    hscr = halo_scratch(cols, chans)

    tangent, lon, send_a, send_b, k0, k1, inv_cells = call(
        edges_kernel,
        [
            full32, lon_shape, send_shape, send_shape, VMEM((layers, 49, 8, 128), F32),
            VMEM((layers, 2, 49, 8, 128), F32), VMEM((layers, rows, cols, 128), F32),
        ],
        [IN_HBM] * 3, (jnp.transpose(perturb, (0, 2, 1)), jnp.transpose(kernels, (1, 2, 0, 3)), inv_std),
        [
            pltpu.VMEM((rows, chans, cols), F32), pltpu.VMEM((7, 7, layers, chans), F32),
            pltpu.VMEM(inv_std.shape, F32), pltpu.SemaphoreType.DMA((rows + 2,)),
        ],
        name="edges",
    )
    side, halo_a, halo_b = exchange(lon, send_a, send_b)
    acc, vv, normed_cells, slope_cells = call(
        first_conv_kernel,
        [full32, sums, VMEM((layers, rows, cols, chans), BF16), VMEM(slope.shape, BF16)],
        [IN_SMEM] + [IN_VMEM] * 5 + [IN_HBM],
        (area, tangent, side, k0, k1, jnp.transpose(normed, (0, 1, 3, 2)), slope),
        kscr + [pltpu.SemaphoreType.DMA((layers,))], conv_flops, "conv_first",
    )
    net = (normed_cells, inv_cells, slope_cells, gains, w_in, across_cells, scales)
    for layer in range(layers):
        last = layer == layers - 1
        outs = [full32, full16, sums] if last else [full32]
        outs = outs + [lon_shape, send_shape, send_shape]
        got = call(
            functools.partial(tangent_kernel, layer, last), outs, [IN_SMEM] + [IN_VMEM] * 13,
            (area, acc, halo_a, halo_b, k0, k1, tangent) + net, hscr, net_flops, f"tangent{layer}",
        )
        side, halo_a, halo_b = exchange(*got[-3:])
        if last:
            grad, back, uu = got[:3]
        else:
            tangent = got[0]
            (acc,) = call(
                functools.partial(conv_kernel, layer + 1, False), [full32], [IN_VMEM] * 4, (tangent, side, k0, k1),
                kscr, conv_flops, f"conv{layer + 1}",
            )
    for layer in range(layers - 1, -1, -1):
        (acc,) = call(
            functools.partial(conv_kernel, layer, True), [full32], [IN_VMEM] * 4, (back, side, k0, k1),
            kscr, conv_flops, f"convt{layer}",
        )
        if layer > 0:
            grad, back, lon, send_a, send_b = call(
                functools.partial(adjoint_kernel, layer - 1), [full32, full16, lon_shape, send_shape, send_shape],
                [IN_VMEM] * 13, (acc, halo_a, halo_b, k0, k1, grad) + net, hscr, net_flops, f"adjoint{layer - 1}",
            )
            side, halo_a, halo_b = exchange(lon, send_a, send_b)
    members = lat_size * lon_size
    w, tile = call(
        final_kernel, [VMEM((rows, chans, cols), F32), VMEM((members, 1, 128), F32)], [IN_SMEM] + [IN_VMEM] * 8,
        (area, acc, halo_a, halo_b, k0, k1, grad, vv, uu), hscr + [pltpu.VMEM((1, chans), F32)], 0, "final",
    )
    tile = lax.all_to_all(tile, ("lat", "lon"), 0, 0, tiled=True)
    new_vec, growth = pl.pallas_call(
        functools.partial(scale_kernel, total),
        out_shape=[jax.ShapeDtypeStruct((rows, chans, cols), F32), jax.ShapeDtypeStruct((1, 128), F32)],
        in_specs=[IN_VMEM, IN_VMEM],
        out_specs=[IN_HBM, IN_VMEM],
        scratch_shapes=[pltpu.VMEM((rows, chans, cols), F32), pltpu.SemaphoreType.DMA((rows,))],
        compiler_params=params(),
        name="scale",
    )(in_vmem(tile), in_vmem(w))
    return jnp.transpose(new_vec, (0, 2, 1)), growth[0, :1]


def solution(mesh):
    in_specs = (
        P(("grp", "lat"), "lon", None),
        P(),
        P(),
        P(),
        P(),
        P(),
        P(None, ("grp", "lat"), "lon", None),
        P(None, ("grp", "lat"), "lon"),
        P(None, ("grp", "lat"), "lon", None),
    )
    out_specs = (P(("grp", "lat"), "lon", None), P("grp"))
    fn = functools.partial(on_device, mesh.shape["lat"], mesh.shape["lon"])
    return jax.shard_map(fn, mesh=mesh, in_specs=in_specs, out_specs=out_specs, check_vma=False)
```

```python
import functools
import math

import jax
import jax.numpy as jnp
import numpy as np
from jax import lax
from jax.experimental import pallas as pl
from jax.experimental.pallas import tpu as pltpu
from jax.sharding import PartitionSpec as P

F32 = jnp.float32
BF16 = jnp.bfloat16
LAT_SPAN = 70.0 * math.pi / 180.0
MARGIN = 8
EXT = 16
VMEM = pltpu.VMEM
ACROSS = (((1,), (1,)), ((), ()))
IN_VMEM = pl.BlockSpec(memory_space=pltpu.VMEM)
IN_HBM = pl.BlockSpec(memory_space=pltpu.HBM)
IN_SMEM = pl.BlockSpec(memory_space=pltpu.SMEM)


def in_vmem(x):
    return pltpu.with_memory_space_constraint(x, pltpu.VMEM)


def tap_index(a, b, flipped):
    return (6 - a) * 7 + (6 - b) if flipped else a * 7 + b


def spread_taps(taps_ref, k0, k1):
    for layer in range(taps_ref.shape[2]):

        def low(index):
            return jnp.broadcast_to(taps_ref[index // 7, index % 7, layer : layer + 1, :128], (8, 128))

        def high(index):
            row = taps_ref[index // 7, index % 7, layer : layer + 1, 128:]
            return jnp.broadcast_to(row, (8, row.shape[1]))

        for a in range(7):
            for b in range(7):
                k0[layer, a * 7 + b] = low(a * 7 + b)
                for flipped in (0, 1):
                    pair = [high(tap_index(a, b, flipped)), high(tap_index(6 - a, b, flipped))]
                    k1[layer, flipped, a * 7 + b] = jnp.concatenate(pair, axis=1)


def planes_kernel(f_ref, x0, x1):
    rows = f_ref.shape[0]
    half = rows // 2

    def load_row(r):
        return f_ref[r].astype(BF16).astype(F32)

    for q in range(half + 3):
        low, high = load_row(q), load_row(rows - 1 - q)
        if q < half:
            x0[q] = low[:, :128]
            x0[rows - 1 - q] = high[:, :128]
        x1[q] = jnp.concatenate([low[:, 128:], high[:, 128:]], axis=1)


def conv_local(x0, x1, lon_ref, k0, k1, layer, out_ref, e0, e1, flipped, beside=None):
    rows, cols, _ = out_ref.shape
    half = rows // 2

    def ends(ref, index, x, side):
        ref[0, index, :MARGIN, :] = side[:MARGIN]
        ref[0, index, MARGIN:, :] = x[index, : 2 * MARGIN, :]
        ref[1, index, : 2 * MARGIN, :] = x[index, cols - 2 * MARGIN :, :]
        ref[1, index, 2 * MARGIN :, :] = side[MARGIN:]

    for r in range(rows):
        ends(e0, r, x0, lon_ref[r, :, :128].astype(F32))
    for q in range(half + 3):
        low, high = lon_ref[q, :, 128:].astype(F32), lon_ref[rows - 1 - q, :, 128:].astype(F32)
        ends(e1, q, x1, jnp.concatenate([low, high], axis=1))

    def tile(base, low_window, high_window):
        acc = [None] * rows
        for b in range(7):
            taps = [k0[layer, tap_index(a, b, flipped)] for a in range(7)]
            for r in range(rows):
                x = low_window(r, b)
                for a in range(7):
                    o = r + 3 - a
                    if 0 <= o < rows:
                        term = taps[a] * x
                        acc[o] = term if acc[o] is None else acc[o] + term
        for o in range(rows):
            out_ref[o, pl.ds(base, 8), :128] = acc[o]
        acc = [None] * half
        for b in range(7):
            taps = [k1[layer, int(flipped), a * 7 + b] for a in range(7)]
            for q in range(half + 3):
                x = high_window(q, b)
                for a in range(7):
                    o = q + 3 - a
                    if 0 <= o < half:
                        term = taps[a] * x
                        acc[o] = term if acc[o] is None else acc[o] + term
        for o in range(half):
            out_ref[o, pl.ds(base, 8), 128:] = acc[o][:, :64]
            out_ref[rows - 1 - o, pl.ds(base, 8), 128:] = acc[o][:, 64:]

    def both(j, *windows):
        tile(pl.multiple_of(j * 8, 8), *windows)
        if beside is not None:
            beside(j)

    last = cols // 8 - 1

    @pl.loop(0, 2)
    def _(s):
        both(
            s * last,
            lambda r, b: e0[s, r, MARGIN - 3 + b : 2 * MARGIN - 3 + b, :],
            lambda q, b: e1[s, q, MARGIN - 3 + b : 2 * MARGIN - 3 + b, :],
        )

    @pl.loop(1, last)
    def _(j):
        base = pl.multiple_of(j * 8, 8)
        both(
            j, lambda r, b: x0[r, pl.ds(base + (b - 3), 8), :], lambda q, b: x1[q, pl.ds(base + (b - 3), 8), :]
        )


def conv_scratch(rows):
    return [
        pltpu.VMEM((2, rows, 3 * MARGIN, 128), F32),
        pltpu.VMEM((2, rows // 2 + 3, 3 * MARGIN, 128), F32),
    ]


def conv_kernel(layer, flipped, x0, x1, lon_ref, k0, k1, out_ref, *scratch):
    conv_local(x0, x1, lon_ref, k0, k1, layer, out_ref, *scratch, flipped)


def first_conv_kernel(
    area_ref, f_ref, x0, x1, lon_ref, k0, k1, turned_ref, slope_hbm, out_ref, sum_ref, normed_out, slope_out, e0, e1, sems
):
    rows, cols, _ = f_ref.shape
    start = lax.axis_index("lat") * rows
    fetches = [
        pltpu.make_async_copy(slope_hbm.at[layer], slope_out.at[layer], sems.at[layer])
        for layer in range(slope_hbm.shape[0])
    ]
    for fetch in fetches:
        fetch.start()
    one = lax.broadcasted_iota(jnp.int32, (cols, cols), 0) == lax.broadcasted_iota(jnp.int32, (cols, cols), 1)
    eye = jnp.where(one, 1.0, 0.0).astype(BF16)

    def turn_row(r):
        x = f_ref[r]
        sum_ref[...] += area_ref[0, start + r] * jnp.sum(x * x, axis=0, keepdims=True)
        for layer in range(turned_ref.shape[0]):
            turned = lax.dot_general(eye, turned_ref[layer, r], ACROSS, preferred_element_type=F32)
            normed_out[layer, r] = turned.astype(BF16)

    sum_ref[...] = jnp.zeros_like(sum_ref)
    steps = cols // 8
    for j in range(steps, rows):
        turn_row(j)

    def beside(j):
        if rows >= steps:
            turn_row(j)
        else:
            pl.when(j < rows)(lambda: turn_row(j))

    conv_local(x0, x1, lon_ref, k0, k1, 0, out_ref, e0, e1, False, beside)
    for fetch in fetches:
        fetch.wait()


def place_halo(parity, a_ref, b_ref, h0, h1):
    width = h0.shape[1]
    cols = width - EXT
    middle = cols // 2
    lane = lax.broadcasted_iota(jnp.int32, (width // 2, 128), 1)
    for e in range(3):
        for ref, first in ((a_ref, (1 - parity) * 3), (b_ref, parity * 3)):
            row = ref[e, :width, :].astype(F32)
            h0[first + e, :MARGIN, :] = row[cols : cols + MARGIN]
            h0[first + e, MARGIN : MARGIN + cols, :] = row[:cols]
            h0[first + e, MARGIN + cols :, :] = row[cols + MARGIN :]
        a_up, a_down = a_ref[e, width:, :].astype(F32), a_ref[2 - e, width:, :].astype(F32)
        b_up, b_down = b_ref[e, width:, :].astype(F32), b_ref[2 - e, width:, :].astype(F32)
        up, down = jnp.where(parity == 1, a_up, b_up), jnp.where(parity == 1, b_down, a_down)
        first = jnp.where(lane < 64, up, pltpu.roll(down, 64, 1))
        second = jnp.where(lane < 64, pltpu.roll(up, 64, 1), down)
        h1[e, :MARGIN, :] = first[middle:]
        h1[e, MARGIN : MARGIN + middle, :] = first[:middle]
        h1[e, MARGIN + middle : MARGIN + cols, :] = second[:middle]
        h1[e, MARGIN + cols :, :] = second[middle:]


def conv_halo(h0, h1, acc_ref, k0, k1, layer, edge, flipped):
    rows, cols, _ = acc_ref.shape
    unroll = 2

    def add(acc, index, term):
        acc[index] = term if acc[index] is None else acc[index] + term

    @pl.loop(0, cols // (8 * unroll))
    def _(block):
        bases = [pl.multiple_of(block * (8 * unroll) + 8 * i, 8) for i in range(unroll)]
        acc = [[None] * 6 for _ in bases]
        for b in range(7):
            taps = {a: k0[layer, tap_index(a, b, flipped)] for a in (0, 1, 2, 4, 5, 6)}
            for i, base in enumerate(bases):
                for e in range(3):
                    upper = h0[e, pl.ds(base + (MARGIN - 3 + b), 8), :]
                    for o in range(e + 1):
                        add(acc[i], o, taps[e - o] * upper)
                    lower = h0[3 + e, pl.ds(base + (MARGIN - 3 + b), 8), :]
                    for p in range(e, 3):
                        add(acc[i], 3 + p, taps[6 + e - p] * lower)
        for i, base in enumerate(bases):
            for o in range(6):
                own = o if o < 3 else rows - 6 + o
                edge[o, pl.ds(base, 8), :128] = acc_ref[own, pl.ds(base, 8), :128] + acc[i][o]
        acc = [[None] * 3 for _ in bases]
        for b in range(7):
            taps = [k1[layer, int(flipped), a * 7 + b] for a in range(3)]
            for i, base in enumerate(bases):
                for e in range(3):
                    both = h1[e, pl.ds(base + (MARGIN - 3 + b), 8), :]
                    for o in range(e + 1):
                        add(acc[i], o, taps[e - o] * both)
        for i, base in enumerate(bases):
            for o in range(3):
                edge[o, pl.ds(base, 8), 128:] = acc_ref[o, pl.ds(base, 8), 128:] + acc[i][o][:, :64]
                own = acc_ref[rows - 1 - o, pl.ds(base, 8), 128:]
                edge[5 - o, pl.ds(base, 8), 128:] = own + acc[i][o][:, 64:]


def halo_scratch(cols, chans):
    return [
        pltpu.VMEM((6, cols + 2 * MARGIN, 128), F32),
        pltpu.VMEM((3, cols + 2 * MARGIN, 128), F32),
        pltpu.VMEM((6, cols, chans), F32),
    ]


def wide(inv, chans):
    return jnp.concatenate([inv, inv[:, : chans - 128]], axis=1)


def project(y, normed, inv):
    chans = y.shape[1]
    normal = normed.astype(F32)
    first = jnp.sum(y, axis=1, keepdims=True) * (1.0 / chans)
    second = jnp.sum(normal * y, axis=1, keepdims=True) * (1.0 / chans)
    return inv * (y - first - normal * second)


def forward_net(y, normed, inv, slope, gain, w_in, w_out_turned, scale):
    operand = (gain * project(y, normed, inv)).astype(BF16)
    hidden = jnp.dot(operand, w_in, preferred_element_type=F32)
    gated = (slope.astype(F32) * hidden).astype(BF16)
    return scale * lax.dot_general(gated, w_out_turned, ACROSS, preferred_element_type=F32)


def adjoint_net(g, normed, inv, slope, gain, w_in, w_out_turned, scale):
    scaled = (scale * g).astype(BF16)
    hidden = jnp.dot(scaled, w_out_turned, preferred_element_type=F32)
    gated = (slope.astype(F32) * hidden).astype(BF16)
    back = lax.dot_general(gated, w_in, ACROSS, preferred_element_type=F32)
    return project(gain * back, normed, inv).astype(BF16)


def fold(values):
    count = values.shape[0] // 2
    return jnp.concatenate([values[:count], values[count:]], axis=1)


def send_rows(parity, field, lon_ref, a_ref, b_ref):
    rows, cols = field.shape[0], field.shape[1]
    width = cols + EXT
    for e in range(3):
        for ref, row in ((a_ref, (1 - parity) * (rows - 3) + e), (b_ref, parity * (rows - 3) + e)):
            ref[e, :cols, :] = field[row, :, :128].astype(BF16)
            ref[e, width : width + cols // 2, :] = fold(field[row, :, 128:].astype(F32)).astype(BF16)
    for r in range(rows):
        lon_ref[r, :MARGIN, :] = field[r, cols - MARGIN :, :].astype(BF16)
        lon_ref[r, MARGIN:, :] = field[r, :MARGIN, :].astype(BF16)


def flat(x):
    return x.reshape(x.shape[0] * x.shape[1], x.shape[2])


class Rows:
    def __init__(self, rows, outer):
        self.spans = [(0, 3), (rows - 3, 3)] if outer else [(3, rows - 6)]

    def get(self, ref, *lead):
        return jnp.concatenate([flat(ref[(*lead, slice(a, a + n))]) for a, n in self.spans], axis=0)

    def put(self, ref, value):
        cols, done = ref.shape[1], 0
        for a, n in self.spans:
            ref[a : a + n] = value[done * cols : (done + n) * cols].reshape(n, cols, value.shape[1])
            done += n

    def numbers(self):
        return [a + i for a, n in self.spans for i in range(n)]


def both_blocks(acc_ref, edge, fn):
    rows = acc_ref.shape[0]
    inner, outer = Rows(rows, False), Rows(rows, True)
    fn(outer, flat(edge[...]))
    fn(inner, inner.get(acc_ref))


def net_operands(layer, block, refs):
    normed_ref, inv_ref, slope_ref, gain_ref, win_ref, wout_ref, scale_ref = refs
    return [
        block.get(normed_ref, layer), wide(block.get(inv_ref, layer), normed_ref.shape[3]), block.get(slope_ref, layer),
        gain_ref[layer : layer + 1, :], win_ref[layer], wout_ref[layer], scale_ref[layer : layer + 1, :],
    ]


def tangent_kernel(layer, last, area_ref, acc_ref, a_ref, b_ref, k0, k1, t_ref, *rest):
    net, rest = rest[:7], rest[7:]
    rows, cols, chans = acc_ref.shape
    lat = lax.axis_index("lat")
    if last:
        g_ref, db_ref, sum_ref, lon_ref, sa_ref, sb_ref, h0, h1, edge = rest
        sum_ref[...] = jnp.zeros_like(sum_ref)
    else:
        t_out, lon_ref, sa_ref, sb_ref, h0, h1, edge = rest
    place_halo(lat % 2, a_ref, b_ref, h0, h1)
    conv_halo(h0, h1, acc_ref, k0, k1, layer, edge, False)

    def work(block, y):
        operands = net_operands(layer, block, net)
        t = block.get(t_ref) + forward_net(y, *operands)
        if not last:
            block.put(t_out, t)
            return
        parts = []
        for i, r in enumerate(block.numbers()):
            u = t[i * cols : (i + 1) * cols]
            g = area_ref[0, lat * rows + r] * u
            sum_ref[...] += jnp.sum(g * u, axis=0, keepdims=True)
            parts.append(g)
        g = jnp.concatenate(parts, axis=0)
        block.put(g_ref, g)
        block.put(db_ref, adjoint_net(g, *operands))

    both_blocks(acc_ref, edge, work)
    send_rows(lat % 2, db_ref if last else t_out, lon_ref, sa_ref, sb_ref)


def adjoint_kernel(layer, acc_ref, a_ref, b_ref, k0, k1, g_ref, *rest):
    net, (g_out, db_ref, lon_ref, sa_ref, sb_ref, h0, h1, edge) = rest[:7], rest[7:]
    parity = lax.axis_index("lat") % 2
    place_halo(parity, a_ref, b_ref, h0, h1)
    conv_halo(h0, h1, acc_ref, k0, k1, layer + 1, edge, True)

    def work(block, y):
        g = block.get(g_ref) + y
        block.put(g_out, g)
        block.put(db_ref, adjoint_net(g, *net_operands(layer, block, net)))

    both_blocks(acc_ref, edge, work)
    send_rows(parity, db_ref, lon_ref, sa_ref, sb_ref)


def final_kernel(
    area_ref, acc_ref, a_ref, b_ref, k0, k1, g_ref, vv_ref, uu_ref, w_ref, tile_ref, h0, h1, edge, ww
):
    rows = acc_ref.shape[0]
    lat = lax.axis_index("lat")
    place_halo(lat % 2, a_ref, b_ref, h0, h1)
    conv_halo(h0, h1, acc_ref, k0, k1, 0, edge, True)
    ww[...] = jnp.zeros_like(ww)

    def row(r, y):
        g = g_ref[r] + y
        w = g * area_ref[1, lat * rows + r]
        w_ref[r] = jnp.transpose(w)
        ww[...] += jnp.sum(g * w, axis=0, keepdims=True)

    for e in range(3):
        row(e, edge[e])
        row(rows - 3 + e, edge[3 + e])

    for r in range(3, rows - 3):
        row(r, acc_ref[r])

    which = lax.broadcasted_iota(jnp.int32, (1, 128), 1)
    vv, uu, wv = (jnp.sum(ref[...]) for ref in (vv_ref, uu_ref, ww))
    tile = jnp.where(which == 0, vv, jnp.where(which == 1, uu, jnp.where(which == 2, wv, 0.0)))
    for i in range(tile_ref.shape[0]):
        tile_ref[i] = tile


def scale_kernel(total, tile_ref, w_ref, out_hbm, growth_ref, scaled, sems):
    sums = jnp.sum(tile_ref[...], axis=0) * (1.0 / total)
    vv, uu, ww = (jnp.broadcast_to(sums[:, i : i + 1], (1, 128)) for i in range(3))
    growth_ref[...] = jnp.sqrt(uu / (vv + 1e-06))
    factor = 1.0 / jnp.sqrt(ww + 1e-06)
    copies = []
    for r in range(w_ref.shape[0]):
        scaled[r] = w_ref[r] * factor
        copies.append(pltpu.make_async_copy(scaled.at[r], out_hbm.at[r], sems.at[r]))
        copies[-1].start()
    for copy in copies:
        copy.wait()


def extend_kernel(after_ref, lon_ref, sa_in, sb_in, sa_ref, sb_ref):
    rows, width = lon_ref.shape[0], sa_ref.shape[1] // 3 * 2
    cols = width - EXT
    parity = lax.axis_index("lat") % 2
    for e in range(3):
        for source, ref, row in (
            (sa_in, sa_ref, (1 - parity) * (rows - 3) + e), (sb_in, sb_ref, parity * (rows - 3) + e)
        ):
            ref[e, :cols, :] = source[e, :cols, :]
            ref[e, width : width + cols // 2, :] = source[e, width : width + cols // 2, :]
            side = lon_ref[row]
            ref[e, cols:width, :] = side[:, :128]
            ref[e, width + cols // 2 :, :] = fold(side[:, 128:].astype(F32)).astype(BF16)


def edges_kernel(
    turned_hbm, taps_hbm, inv_hbm, t_ref, lon_ref, sa_ref, sb_ref, k0, k1, inv_out, turned, taps_ref, inv_ref, sems
):
    rows = turned.shape[0]
    copies = [pltpu.make_async_copy(turned_hbm.at[r], turned.at[r], sems.at[r]) for r in range(rows)]
    small = [
        pltpu.make_async_copy(inv_hbm, inv_ref, sems.at[rows]),
        pltpu.make_async_copy(taps_hbm, taps_ref, sems.at[rows + 1]),
    ]
    for copy in small + copies:
        copy.start()
    for copy in small:
        copy.wait()
    spread_taps(taps_ref, k0, k1)
    for layer in range(inv_ref.shape[0]):
        for r in range(rows):
            inv = jnp.broadcast_to(inv_ref[layer, r : r + 1, :], (128, inv_ref.shape[2]))
            inv_out[layer, r] = jnp.transpose(inv)
    for r, copy in enumerate(copies):
        copy.wait()
        t_ref[r] = jnp.transpose(turned[r])
    send_rows(lax.axis_index("lat") % 2, t_ref, lon_ref, sa_ref, sb_ref)


def params():
    return pltpu.CompilerParams(vmem_limit_bytes=16 * 1024 * 1024)


def on_device(lat_size, lon_size, perturb, kernels, gains, w_in, w_out, scales, normed, inv_std, slope):
    rows, cols, chans = perturb.shape
    hidden = w_in.shape[2]
    layers = kernels.shape[0]
    lat_total = rows * lat_size
    angles = LAT_SPAN * (np.arange(lat_total) + 0.5) / lat_total
    total = float(np.sum(np.cos(angles))) * cols * lon_size * chans
    table = np.stack([np.cos(angles), 1.0 / np.cos(angles)]).astype(np.float32)
    area = jnp.asarray(table)
    across_cells = jnp.transpose(w_out, (0, 2, 1))
    swap_a = [(i, i ^ 1) for i in range(lat_size) if i ^ 1 < lat_size]
    swap_b = [pair for i in range(1, lat_size - 1, 2) for pair in ((i, i + 1), (i + 1, i))]
    swap_lon = [(i, (i + 1) % lon_size) for i in range(lon_size)]

    lon_shape = VMEM((rows, EXT, chans), BF16)
    send_shape = VMEM((3, (cols + EXT) // 2 * 3, 128), BF16)
    full32 = VMEM((rows, cols, chans), F32)
    full16 = VMEM((rows, cols, chans), BF16)
    sums = VMEM((1, chans), F32)

    def call(kernel, out_shape, in_specs, args, scratch=(), flops=0, name=None):
        args = [pltpu.with_memory_space_constraint(x, spec.memory_space) if spec is not IN_SMEM else x for spec, x in zip(in_specs, args)]
        return pl.pallas_call(
            kernel,
            out_shape=out_shape,
            in_specs=in_specs,
            out_specs=[IN_VMEM] * len(out_shape),
            scratch_shapes=list(scratch),
            compiler_params=params(),
            cost_estimate=pl.CostEstimate(flops=flops, bytes_accessed=4_000_000, transcendentals=0),
            name=name,
        )(*args)

    def exchange(field, lon, send_a, send_b):
        side = lax.ppermute(lon, "lon", swap_lon)
        planes = call(
            planes_kernel, [VMEM((rows, cols, 128), F32), VMEM((rows // 2 + 3, cols, 128), F32)], [IN_VMEM], (field,),
            flops=conv_flops // 8, name="planes",
        )
        send_a, send_b = call(
            extend_kernel, [send_shape] * 2, [IN_VMEM] * 4, (planes[1], side, send_a, send_b), name="extend"
        )
        halo_b = lax.ppermute(send_b, "lat", swap_b)
        halo_a = lax.ppermute(send_a, "lat", swap_a)
        return (*planes, side), halo_a, halo_b

    conv_flops = 2 * 49 * rows * cols * chans
    net_flops = 4 * rows * cols * chans * hidden
    kscr = conv_scratch(rows)
    hscr = halo_scratch(cols, chans)

    tangent, lon, send_a, send_b, k0, k1, inv_cells = call(
        edges_kernel,
        [
            full32, lon_shape, send_shape, send_shape, VMEM((layers, 49, 8, 128), F32),
            VMEM((layers, 2, 49, 8, 128), F32), VMEM((layers, rows, cols, 128), F32),
        ],
        [IN_HBM] * 3, (jnp.transpose(perturb, (0, 2, 1)), jnp.transpose(kernels, (1, 2, 0, 3)), inv_std),
        [
            pltpu.VMEM((rows, chans, cols), F32), pltpu.VMEM((7, 7, layers, chans), F32),
            pltpu.VMEM(inv_std.shape, F32), pltpu.SemaphoreType.DMA((rows + 2,)),
        ],
        name="edges",
    )
    taken, halo_a, halo_b = exchange(tangent, lon, send_a, send_b)
    acc, vv, normed_cells, slope_cells = call(
        first_conv_kernel,
        [full32, sums, VMEM((layers, rows, cols, chans), BF16), VMEM(slope.shape, BF16)],
        [IN_SMEM] + [IN_VMEM] * 7 + [IN_HBM],
        (area, tangent, *taken, k0, k1, jnp.transpose(normed, (0, 1, 3, 2)), slope),
        kscr + [pltpu.SemaphoreType.DMA((layers,))], conv_flops, "conv_first",
    )
    net = (normed_cells, inv_cells, slope_cells, gains, w_in, across_cells, scales)
    for layer in range(layers):
        last = layer == layers - 1
        outs = [full32, full16, sums] if last else [full32]
        outs = outs + [lon_shape, send_shape, send_shape]
        got = call(
            functools.partial(tangent_kernel, layer, last), outs, [IN_SMEM] + [IN_VMEM] * 13,
            (area, acc, halo_a, halo_b, k0, k1, tangent) + net, hscr, net_flops, f"tangent{layer}",
        )
        if last:
            grad, back, uu = got[:3]
        else:
            tangent = got[0]
        taken, halo_a, halo_b = exchange(back if last else tangent, *got[-3:])
        if not last:
            (acc,) = call(
                functools.partial(conv_kernel, layer + 1, False), [full32], [IN_VMEM] * 5, (*taken, k0, k1),
                kscr, conv_flops, f"conv{layer + 1}",
            )
    for layer in range(layers - 1, -1, -1):
        (acc,) = call(
            functools.partial(conv_kernel, layer, True), [full32], [IN_VMEM] * 5, (*taken, k0, k1),
            kscr, conv_flops, f"convt{layer}",
        )
        if layer > 0:
            grad, back, lon, send_a, send_b = call(
                functools.partial(adjoint_kernel, layer - 1), [full32, full16, lon_shape, send_shape, send_shape],
                [IN_VMEM] * 13, (acc, halo_a, halo_b, k0, k1, grad) + net, hscr, net_flops, f"adjoint{layer - 1}",
            )
            taken, halo_a, halo_b = exchange(back, lon, send_a, send_b)
    members = lat_size * lon_size
    w, tile = call(
        final_kernel, [VMEM((rows, chans, cols), F32), VMEM((members, 1, 128), F32)], [IN_SMEM] + [IN_VMEM] * 8,
        (area, acc, halo_a, halo_b, k0, k1, grad, vv, uu), hscr + [pltpu.VMEM((1, chans), F32)], 0, "final",
    )
    tile = lax.all_to_all(tile, ("lat", "lon"), 0, 0, tiled=True)
    new_vec, growth = pl.pallas_call(
        functools.partial(scale_kernel, total),
        out_shape=[jax.ShapeDtypeStruct((rows, chans, cols), F32), jax.ShapeDtypeStruct((1, 128), F32)],
        in_specs=[IN_VMEM, IN_VMEM],
        out_specs=[IN_HBM, IN_VMEM],
        scratch_shapes=[pltpu.VMEM((rows, chans, cols), F32), pltpu.SemaphoreType.DMA((rows,))],
        compiler_params=params(),
        name="scale",
    )(in_vmem(tile), in_vmem(w))
    return jnp.transpose(new_vec, (0, 2, 1)), growth[0, :1]


def solution(mesh):
    in_specs = (
        P(("grp", "lat"), "lon", None),
        P(),
        P(),
        P(),
        P(),
        P(),
        P(None, ("grp", "lat"), "lon", None),
        P(None, ("grp", "lat"), "lon"),
        P(None, ("grp", "lat"), "lon", None),
    )
    out_specs = (P(("grp", "lat"), "lon", None), P("grp"))
    fn = functools.partial(on_device, mesh.shape["lat"], mesh.shape["lon"])
    return jax.shard_map(fn, mesh=mesh, in_specs=in_specs, out_specs=out_specs, check_vma=False)
```

```python
import functools
import math

import jax
import jax.numpy as jnp
import numpy as np
from jax import lax
from jax.experimental import pallas as pl
from jax.experimental.pallas import tpu as pltpu
from jax.sharding import PartitionSpec as P

F32 = jnp.float32
BF16 = jnp.bfloat16
LAT_SPAN = 70.0 * math.pi / 180.0
MARGIN = 8
EARLY = 2
EXT = 16
VMEM = pltpu.VMEM
ACROSS = (((1,), (1,)), ((), ()))
IN_VMEM = pl.BlockSpec(memory_space=pltpu.VMEM)
IN_HBM = pl.BlockSpec(memory_space=pltpu.HBM)
IN_SMEM = pl.BlockSpec(memory_space=pltpu.SMEM)


def in_vmem(x):
    return pltpu.with_memory_space_constraint(x, pltpu.VMEM)


def tap_index(a, b, flipped):
    return (6 - a) * 7 + (6 - b) if flipped else a * 7 + b


def spread_taps(taps_ref, k0, k1):
    for layer in range(taps_ref.shape[2]):

        def low(index):
            return jnp.broadcast_to(taps_ref[index // 7, index % 7, layer : layer + 1, :128], (8, 128))

        def high(index):
            row = taps_ref[index // 7, index % 7, layer : layer + 1, 128:]
            return jnp.broadcast_to(row, (8, row.shape[1]))

        for a in range(7):
            for b in range(7):
                k0[layer, a * 7 + b] = low(a * 7 + b)
                for flipped in (0, 1):
                    pair = [high(tap_index(a, b, flipped)), high(tap_index(6 - a, b, flipped))]
                    k1[layer, flipped, a * 7 + b] = jnp.concatenate(pair, axis=1)


def tap_tile(k0, k1, layer, flipped, rows, out_ref, base, low_window, high_window):
    half = rows // 2
    acc = [None] * rows
    for b in range(7):
        taps = [k0[layer, tap_index(a, b, flipped)] for a in range(7)]
        for r in range(rows):
            x = low_window(r, b)
            for a in range(7):
                o = r + 3 - a
                if 0 <= o < rows:
                    term = taps[a] * x
                    acc[o] = term if acc[o] is None else acc[o] + term
    for o in range(rows):
        out_ref[o, pl.ds(base, 8), :128] = acc[o]
    acc = [None] * half
    for b in range(7):
        taps = [k1[layer, int(flipped), a * 7 + b] for a in range(7)]
        for q in range(half + 3):
            x = high_window(q, b)
            for a in range(7):
                o = q + 3 - a
                if 0 <= o < half:
                    term = taps[a] * x
                    acc[o] = term if acc[o] is None else acc[o] + term
    for o in range(half):
        out_ref[o, pl.ds(base, 8), 128:] = acc[o][:, :64]
        out_ref[rows - 1 - o, pl.ds(base, 8), 128:] = acc[o][:, 64:]


def plane_windows(x0, x1, base):
    return (
        lambda r, b: x0[r, pl.ds(base + (b - 3), 8), :],
        lambda q, b: x1[q, pl.ds(base + (b - 3), 8), :],
    )


def planes_kernel(layer, flipped, f_ref, k0, k1, x0, x1, early_ref):
    rows = f_ref.shape[0]
    half = rows // 2

    def load_row(r):
        return f_ref[r].astype(BF16).astype(F32)

    for q in range(half + 3):
        low, high = load_row(q), load_row(rows - 1 - q)
        if q < half:
            x0[q] = low[:, :128]
            x0[rows - 1 - q] = high[:, :128]
        x1[q] = jnp.concatenate([low[:, 128:], high[:, 128:]], axis=1)

    @pl.loop(0, EARLY)
    def _(j):
        base = pl.multiple_of(j * 8, 8)
        tap_tile(k0, k1, layer, flipped, rows, early_ref, base, *plane_windows(x0, x1, base + 8))


def conv_local(x0, x1, early_ref, lon_ref, k0, k1, layer, out_ref, e0, e1, flipped, beside=None):
    rows, cols, _ = out_ref.shape
    half = rows // 2

    def ends(ref, index, x, side):
        ref[0, index, :MARGIN, :] = side[:MARGIN]
        ref[0, index, MARGIN:, :] = x[index, : 2 * MARGIN, :]
        ref[1, index, : 2 * MARGIN, :] = x[index, cols - 2 * MARGIN :, :]
        ref[1, index, 2 * MARGIN :, :] = side[MARGIN:]

    for r in range(rows):
        ends(e0, r, x0, lon_ref[r, :, :128].astype(F32))
    for q in range(half + 3):
        low, high = lon_ref[q, :, 128:].astype(F32), lon_ref[rows - 1 - q, :, 128:].astype(F32)
        ends(e1, q, x1, jnp.concatenate([low, high], axis=1))

    def both(j, *windows):
        tap_tile(k0, k1, layer, flipped, rows, out_ref, pl.multiple_of(j * 8, 8), *windows)
        if beside is not None:
            beside(j)

    last = cols // 8 - 1

    @pl.loop(0, 2)
    def _(s):
        both(
            s * last,
            lambda r, b: e0[s, r, MARGIN - 3 + b : 2 * MARGIN - 3 + b, :],
            lambda q, b: e1[s, q, MARGIN - 3 + b : 2 * MARGIN - 3 + b, :],
        )

    for r in range(rows):
        out_ref[r, 8 : 8 + 8 * EARLY, :] = early_ref[r]
    if beside is not None:
        for j in range(1, 1 + EARLY):
            beside(j)

    @pl.loop(1 + EARLY, last)
    def _(j):
        both(j, *plane_windows(x0, x1, pl.multiple_of(j * 8, 8)))


def conv_scratch(rows):
    return [
        pltpu.VMEM((2, rows, 3 * MARGIN, 128), F32),
        pltpu.VMEM((2, rows // 2 + 3, 3 * MARGIN, 128), F32),
    ]


def conv_kernel(layer, flipped, x0, x1, early_ref, lon_ref, k0, k1, out_ref, *scratch):
    conv_local(x0, x1, early_ref, lon_ref, k0, k1, layer, out_ref, *scratch, flipped)


def first_conv_kernel(
    area_ref, f_ref, x0, x1, early_ref, lon_ref, k0, k1, turned_ref, slope_hbm, out_ref, sum_ref, normed_out, slope_out, e0, e1, sems
):
    rows, cols, _ = f_ref.shape
    start = lax.axis_index("lat") * rows
    fetches = [
        pltpu.make_async_copy(slope_hbm.at[layer], slope_out.at[layer], sems.at[layer])
        for layer in range(slope_hbm.shape[0])
    ]
    for fetch in fetches:
        fetch.start()
    one = lax.broadcasted_iota(jnp.int32, (cols, cols), 0) == lax.broadcasted_iota(jnp.int32, (cols, cols), 1)
    eye = jnp.where(one, 1.0, 0.0).astype(BF16)

    def turn_row(r):
        x = f_ref[r]
        sum_ref[...] += area_ref[0, start + r] * jnp.sum(x * x, axis=0, keepdims=True)
        for layer in range(turned_ref.shape[0]):
            turned = lax.dot_general(eye, turned_ref[layer, r], ACROSS, preferred_element_type=F32)
            normed_out[layer, r] = turned.astype(BF16)

    sum_ref[...] = jnp.zeros_like(sum_ref)
    steps = cols // 8
    for j in range(steps, rows):
        turn_row(j)

    def beside(j):
        if rows >= steps:
            turn_row(j)
        else:
            pl.when(j < rows)(lambda: turn_row(j))

    conv_local(x0, x1, early_ref, lon_ref, k0, k1, 0, out_ref, e0, e1, False, beside)
    for fetch in fetches:
        fetch.wait()


def place_halo(parity, a_ref, b_ref, h0, h1):
    width = h0.shape[1]
    cols = width - EXT
    middle = cols // 2
    lane = lax.broadcasted_iota(jnp.int32, (width // 2, 128), 1)
    for e in range(3):
        for ref, first in ((a_ref, (1 - parity) * 3), (b_ref, parity * 3)):
            row = ref[e, :width, :].astype(F32)
            h0[first + e, :MARGIN, :] = row[cols : cols + MARGIN]
            h0[first + e, MARGIN : MARGIN + cols, :] = row[:cols]
            h0[first + e, MARGIN + cols :, :] = row[cols + MARGIN :]
        a_up, a_down = a_ref[e, width:, :].astype(F32), a_ref[2 - e, width:, :].astype(F32)
        b_up, b_down = b_ref[e, width:, :].astype(F32), b_ref[2 - e, width:, :].astype(F32)
        up, down = jnp.where(parity == 1, a_up, b_up), jnp.where(parity == 1, b_down, a_down)
        first = jnp.where(lane < 64, up, pltpu.roll(down, 64, 1))
        second = jnp.where(lane < 64, pltpu.roll(up, 64, 1), down)
        h1[e, :MARGIN, :] = first[middle:]
        h1[e, MARGIN : MARGIN + middle, :] = first[:middle]
        h1[e, MARGIN + middle : MARGIN + cols, :] = second[:middle]
        h1[e, MARGIN + cols :, :] = second[middle:]


def conv_halo(h0, h1, acc_ref, k0, k1, layer, edge, flipped):
    rows, cols, _ = acc_ref.shape
    unroll = 2

    def add(acc, index, term):
        acc[index] = term if acc[index] is None else acc[index] + term

    @pl.loop(0, cols // (8 * unroll))
    def _(block):
        bases = [pl.multiple_of(block * (8 * unroll) + 8 * i, 8) for i in range(unroll)]
        acc = [[None] * 6 for _ in bases]
        for b in range(7):
            taps = {a: k0[layer, tap_index(a, b, flipped)] for a in (0, 1, 2, 4, 5, 6)}
            for i, base in enumerate(bases):
                for e in range(3):
                    upper = h0[e, pl.ds(base + (MARGIN - 3 + b), 8), :]
                    for o in range(e + 1):
                        add(acc[i], o, taps[e - o] * upper)
                    lower = h0[3 + e, pl.ds(base + (MARGIN - 3 + b), 8), :]
                    for p in range(e, 3):
                        add(acc[i], 3 + p, taps[6 + e - p] * lower)
        for i, base in enumerate(bases):
            for o in range(6):
                own = o if o < 3 else rows - 6 + o
                edge[o, pl.ds(base, 8), :128] = acc_ref[own, pl.ds(base, 8), :128] + acc[i][o]
        acc = [[None] * 3 for _ in bases]
        for b in range(7):
            taps = [k1[layer, int(flipped), a * 7 + b] for a in range(3)]
            for i, base in enumerate(bases):
                for e in range(3):
                    both = h1[e, pl.ds(base + (MARGIN - 3 + b), 8), :]
                    for o in range(e + 1):
                        add(acc[i], o, taps[e - o] * both)
        for i, base in enumerate(bases):
            for o in range(3):
                edge[o, pl.ds(base, 8), 128:] = acc_ref[o, pl.ds(base, 8), 128:] + acc[i][o][:, :64]
                own = acc_ref[rows - 1 - o, pl.ds(base, 8), 128:]
                edge[5 - o, pl.ds(base, 8), 128:] = own + acc[i][o][:, 64:]


def halo_scratch(cols, chans):
    return [
        pltpu.VMEM((6, cols + 2 * MARGIN, 128), F32),
        pltpu.VMEM((3, cols + 2 * MARGIN, 128), F32),
        pltpu.VMEM((6, cols, chans), F32),
    ]


def wide(inv, chans):
    return jnp.concatenate([inv, inv[:, : chans - 128]], axis=1)


def project(y, normed, inv):
    chans = y.shape[1]
    normal = normed.astype(F32)
    first = jnp.sum(y, axis=1, keepdims=True) * (1.0 / chans)
    second = jnp.sum(normal * y, axis=1, keepdims=True) * (1.0 / chans)
    return inv * (y - first - normal * second)


def forward_net(y, normed, inv, slope, gain, w_in, w_out_turned, scale):
    operand = (gain * project(y, normed, inv)).astype(BF16)
    hidden = jnp.dot(operand, w_in, preferred_element_type=F32)
    gated = (slope.astype(F32) * hidden).astype(BF16)
    return scale * lax.dot_general(gated, w_out_turned, ACROSS, preferred_element_type=F32)


def adjoint_net(g, normed, inv, slope, gain, w_in, w_out_turned, scale):
    scaled = (scale * g).astype(BF16)
    hidden = jnp.dot(scaled, w_out_turned, preferred_element_type=F32)
    gated = (slope.astype(F32) * hidden).astype(BF16)
    back = lax.dot_general(gated, w_in, ACROSS, preferred_element_type=F32)
    return project(gain * back, normed, inv).astype(BF16)


def fold(values):
    count = values.shape[0] // 2
    return jnp.concatenate([values[:count], values[count:]], axis=1)


def send_rows(parity, field, lon_ref, a_ref, b_ref):
    rows, cols = field.shape[0], field.shape[1]
    width = cols + EXT
    for e in range(3):
        for ref, row in ((a_ref, (1 - parity) * (rows - 3) + e), (b_ref, parity * (rows - 3) + e)):
            ref[e, :cols, :] = field[row, :, :128].astype(BF16)
            ref[e, width : width + cols // 2, :] = fold(field[row, :, 128:].astype(F32)).astype(BF16)
    for r in range(rows):
        lon_ref[r, :MARGIN, :] = field[r, cols - MARGIN :, :].astype(BF16)
        lon_ref[r, MARGIN:, :] = field[r, :MARGIN, :].astype(BF16)


def flat(x):
    return x.reshape(x.shape[0] * x.shape[1], x.shape[2])


class Rows:
    def __init__(self, rows, outer):
        self.spans = [(0, 3), (rows - 3, 3)] if outer else [(3, rows - 6)]

    def get(self, ref, *lead):
        return jnp.concatenate([flat(ref[(*lead, slice(a, a + n))]) for a, n in self.spans], axis=0)

    def put(self, ref, value):
        cols, done = ref.shape[1], 0
        for a, n in self.spans:
            ref[a : a + n] = value[done * cols : (done + n) * cols].reshape(n, cols, value.shape[1])
            done += n

    def numbers(self):
        return [a + i for a, n in self.spans for i in range(n)]


def both_blocks(acc_ref, edge, fn):
    rows = acc_ref.shape[0]
    inner, outer = Rows(rows, False), Rows(rows, True)
    fn(outer, flat(edge[...]))
    fn(inner, inner.get(acc_ref))


def net_operands(layer, block, refs):
    normed_ref, inv_ref, slope_ref, gain_ref, win_ref, wout_ref, scale_ref = refs
    return [
        block.get(normed_ref, layer), wide(block.get(inv_ref, layer), normed_ref.shape[3]), block.get(slope_ref, layer),
        gain_ref[layer : layer + 1, :], win_ref[layer], wout_ref[layer], scale_ref[layer : layer + 1, :],
    ]


def tangent_kernel(layer, last, area_ref, acc_ref, a_ref, b_ref, k0, k1, t_ref, *rest):
    net, rest = rest[:7], rest[7:]
    rows, cols, chans = acc_ref.shape
    lat = lax.axis_index("lat")
    if last:
        g_ref, db_ref, sum_ref, lon_ref, sa_ref, sb_ref, h0, h1, edge = rest
        sum_ref[...] = jnp.zeros_like(sum_ref)
    else:
        t_out, lon_ref, sa_ref, sb_ref, h0, h1, edge = rest
    place_halo(lat % 2, a_ref, b_ref, h0, h1)
    conv_halo(h0, h1, acc_ref, k0, k1, layer, edge, False)

    def work(block, y):
        operands = net_operands(layer, block, net)
        t = block.get(t_ref) + forward_net(y, *operands)
        if not last:
            block.put(t_out, t)
            return
        parts = []
        for i, r in enumerate(block.numbers()):
            u = t[i * cols : (i + 1) * cols]
            g = area_ref[0, lat * rows + r] * u
            sum_ref[...] += jnp.sum(g * u, axis=0, keepdims=True)
            parts.append(g)
        g = jnp.concatenate(parts, axis=0)
        block.put(g_ref, g)
        block.put(db_ref, adjoint_net(g, *operands))

    both_blocks(acc_ref, edge, work)
    send_rows(lat % 2, db_ref if last else t_out, lon_ref, sa_ref, sb_ref)


def adjoint_kernel(layer, acc_ref, a_ref, b_ref, k0, k1, g_ref, *rest):
    net, (g_out, db_ref, lon_ref, sa_ref, sb_ref, h0, h1, edge) = rest[:7], rest[7:]
    parity = lax.axis_index("lat") % 2
    place_halo(parity, a_ref, b_ref, h0, h1)
    conv_halo(h0, h1, acc_ref, k0, k1, layer + 1, edge, True)

    def work(block, y):
        g = block.get(g_ref) + y
        block.put(g_out, g)
        block.put(db_ref, adjoint_net(g, *net_operands(layer, block, net)))

    both_blocks(acc_ref, edge, work)
    send_rows(parity, db_ref, lon_ref, sa_ref, sb_ref)


def final_kernel(
    area_ref, acc_ref, a_ref, b_ref, k0, k1, g_ref, vv_ref, uu_ref, w_ref, tile_ref, h0, h1, edge, ww
):
    rows = acc_ref.shape[0]
    lat = lax.axis_index("lat")
    place_halo(lat % 2, a_ref, b_ref, h0, h1)
    conv_halo(h0, h1, acc_ref, k0, k1, 0, edge, True)
    ww[...] = jnp.zeros_like(ww)

    def row(r, y):
        g = g_ref[r] + y
        w = g * area_ref[1, lat * rows + r]
        w_ref[r] = jnp.transpose(w)
        ww[...] += jnp.sum(g * w, axis=0, keepdims=True)

    for e in range(3):
        row(e, edge[e])
        row(rows - 3 + e, edge[3 + e])

    for r in range(3, rows - 3):
        row(r, acc_ref[r])

    which = lax.broadcasted_iota(jnp.int32, (1, 128), 1)
    vv, uu, wv = (jnp.sum(ref[...]) for ref in (vv_ref, uu_ref, ww))
    tile = jnp.where(which == 0, vv, jnp.where(which == 1, uu, jnp.where(which == 2, wv, 0.0)))
    for i in range(tile_ref.shape[0]):
        tile_ref[i] = tile


def scale_kernel(total, tile_ref, w_ref, out_hbm, growth_ref, scaled, sems):
    sums = jnp.sum(tile_ref[...], axis=0) * (1.0 / total)
    vv, uu, ww = (jnp.broadcast_to(sums[:, i : i + 1], (1, 128)) for i in range(3))
    growth_ref[...] = jnp.sqrt(uu / (vv + 1e-06))
    factor = 1.0 / jnp.sqrt(ww + 1e-06)
    copies = []
    for r in range(w_ref.shape[0]):
        scaled[r] = w_ref[r] * factor
        copies.append(pltpu.make_async_copy(scaled.at[r], out_hbm.at[r], sems.at[r]))
        copies[-1].start()
    for copy in copies:
        copy.wait()


def extend_kernel(after_ref, lon_ref, sa_in, sb_in, sa_ref, sb_ref):
    rows, width = lon_ref.shape[0], sa_ref.shape[1] // 3 * 2
    cols = width - EXT
    parity = lax.axis_index("lat") % 2
    for e in range(3):
        for source, ref, row in (
            (sa_in, sa_ref, (1 - parity) * (rows - 3) + e), (sb_in, sb_ref, parity * (rows - 3) + e)
        ):
            ref[e, :cols, :] = source[e, :cols, :]
            ref[e, width : width + cols // 2, :] = source[e, width : width + cols // 2, :]
            side = lon_ref[row]
            ref[e, cols:width, :] = side[:, :128]
            ref[e, width + cols // 2 :, :] = fold(side[:, 128:].astype(F32)).astype(BF16)


def edges_kernel(
    turned_hbm, taps_hbm, inv_hbm, t_ref, lon_ref, sa_ref, sb_ref, k0, k1, inv_out, turned, taps_ref, inv_ref, sems
):
    rows = turned.shape[0]
    copies = [pltpu.make_async_copy(turned_hbm.at[r], turned.at[r], sems.at[r]) for r in range(rows)]
    small = [
        pltpu.make_async_copy(inv_hbm, inv_ref, sems.at[rows]),
        pltpu.make_async_copy(taps_hbm, taps_ref, sems.at[rows + 1]),
    ]
    for copy in small + copies:
        copy.start()
    for copy in small:
        copy.wait()
    spread_taps(taps_ref, k0, k1)
    for layer in range(inv_ref.shape[0]):
        for r in range(rows):
            inv = jnp.broadcast_to(inv_ref[layer, r : r + 1, :], (128, inv_ref.shape[2]))
            inv_out[layer, r] = jnp.transpose(inv)
    for r, copy in enumerate(copies):
        copy.wait()
        t_ref[r] = jnp.transpose(turned[r])
    send_rows(lax.axis_index("lat") % 2, t_ref, lon_ref, sa_ref, sb_ref)


def params():
    return pltpu.CompilerParams(vmem_limit_bytes=16 * 1024 * 1024)


def on_device(lat_size, lon_size, perturb, kernels, gains, w_in, w_out, scales, normed, inv_std, slope):
    rows, cols, chans = perturb.shape
    hidden = w_in.shape[2]
    layers = kernels.shape[0]
    lat_total = rows * lat_size
    angles = LAT_SPAN * (np.arange(lat_total) + 0.5) / lat_total
    total = float(np.sum(np.cos(angles))) * cols * lon_size * chans
    table = np.stack([np.cos(angles), 1.0 / np.cos(angles)]).astype(np.float32)
    area = jnp.asarray(table)
    across_cells = jnp.transpose(w_out, (0, 2, 1))
    swap_a = [(i, i ^ 1) for i in range(lat_size) if i ^ 1 < lat_size]
    swap_b = [pair for i in range(1, lat_size - 1, 2) for pair in ((i, i + 1), (i + 1, i))]
    swap_lon = [(i, (i + 1) % lon_size) for i in range(lon_size)]

    lon_shape = VMEM((rows, EXT, chans), BF16)
    send_shape = VMEM((3, (cols + EXT) // 2 * 3, 128), BF16)
    full32 = VMEM((rows, cols, chans), F32)
    full16 = VMEM((rows, cols, chans), BF16)
    sums = VMEM((1, chans), F32)

    def call(kernel, out_shape, in_specs, args, scratch=(), flops=0, name=None):
        args = [pltpu.with_memory_space_constraint(x, spec.memory_space) if spec is not IN_SMEM else x for spec, x in zip(in_specs, args)]
        return pl.pallas_call(
            kernel,
            out_shape=out_shape,
            in_specs=in_specs,
            out_specs=[IN_VMEM] * len(out_shape),
            scratch_shapes=list(scratch),
            compiler_params=params(),
            cost_estimate=pl.CostEstimate(flops=flops, bytes_accessed=4_000_000, transcendentals=0),
            name=name,
        )(*args)

    def exchange(layer, flipped, field, lon, send_a, send_b):
        side = lax.ppermute(lon, "lon", swap_lon)
        planes = call(
            functools.partial(planes_kernel, layer, flipped),
            [
                VMEM((rows, cols, 128), F32), VMEM((rows // 2 + 3, cols, 128), F32),
                VMEM((rows, 8 * EARLY, chans), F32),
            ],
            [IN_VMEM] * 3, (field, k0, k1),
            flops=conv_flops // 8, name="planes",
        )
        send_a, send_b = call(
            extend_kernel, [send_shape] * 2, [IN_VMEM] * 4, (planes[2], side, send_a, send_b), name="extend"
        )
        halo_b = lax.ppermute(send_b, "lat", swap_b)
        halo_a = lax.ppermute(send_a, "lat", swap_a)
        return (*planes, side), halo_a, halo_b

    conv_flops = 2 * 49 * rows * cols * chans
    net_flops = 4 * rows * cols * chans * hidden
    kscr = conv_scratch(rows)
    hscr = halo_scratch(cols, chans)

    tangent, lon, send_a, send_b, k0, k1, inv_cells = call(
        edges_kernel,
        [
            full32, lon_shape, send_shape, send_shape, VMEM((layers, 49, 8, 128), F32),
            VMEM((layers, 2, 49, 8, 128), F32), VMEM((layers, rows, cols, 128), F32),
        ],
        [IN_HBM] * 3, (jnp.transpose(perturb, (0, 2, 1)), jnp.transpose(kernels, (1, 2, 0, 3)), inv_std),
        [
            pltpu.VMEM((rows, chans, cols), F32), pltpu.VMEM((7, 7, layers, chans), F32),
            pltpu.VMEM(inv_std.shape, F32), pltpu.SemaphoreType.DMA((rows + 2,)),
        ],
        name="edges",
    )
    taken, halo_a, halo_b = exchange(0, False, tangent, lon, send_a, send_b)
    acc, vv, normed_cells, slope_cells = call(
        first_conv_kernel,
        [full32, sums, VMEM((layers, rows, cols, chans), BF16), VMEM(slope.shape, BF16)],
        [IN_SMEM] + [IN_VMEM] * 8 + [IN_HBM],
        (area, tangent, *taken, k0, k1, jnp.transpose(normed, (0, 1, 3, 2)), slope),
        kscr + [pltpu.SemaphoreType.DMA((layers,))], conv_flops, "conv_first",
    )
    net = (normed_cells, inv_cells, slope_cells, gains, w_in, across_cells, scales)
    for layer in range(layers):
        last = layer == layers - 1
        outs = [full32, full16, sums] if last else [full32]
        outs = outs + [lon_shape, send_shape, send_shape]
        got = call(
            functools.partial(tangent_kernel, layer, last), outs, [IN_SMEM] + [IN_VMEM] * 13,
            (area, acc, halo_a, halo_b, k0, k1, tangent) + net, hscr, net_flops, f"tangent{layer}",
        )
        if last:
            grad, back, uu = got[:3]
        else:
            tangent = got[0]
        taken, halo_a, halo_b = exchange(layer + (not last), last, back if last else tangent, *got[-3:])
        if not last:
            (acc,) = call(
                functools.partial(conv_kernel, layer + 1, False), [full32], [IN_VMEM] * 6, (*taken, k0, k1),
                kscr, conv_flops, f"conv{layer + 1}",
            )
    for layer in range(layers - 1, -1, -1):
        (acc,) = call(
            functools.partial(conv_kernel, layer, True), [full32], [IN_VMEM] * 6, (*taken, k0, k1),
            kscr, conv_flops, f"convt{layer}",
        )
        if layer > 0:
            grad, back, lon, send_a, send_b = call(
                functools.partial(adjoint_kernel, layer - 1), [full32, full16, lon_shape, send_shape, send_shape],
                [IN_VMEM] * 13, (acc, halo_a, halo_b, k0, k1, grad) + net, hscr, net_flops, f"adjoint{layer - 1}",
            )
            taken, halo_a, halo_b = exchange(layer - 1, True, back, lon, send_a, send_b)
    members = lat_size * lon_size
    w, tile = call(
        final_kernel, [VMEM((rows, chans, cols), F32), VMEM((members, 1, 128), F32)], [IN_SMEM] + [IN_VMEM] * 8,
        (area, acc, halo_a, halo_b, k0, k1, grad, vv, uu), hscr + [pltpu.VMEM((1, chans), F32)], 0, "final",
    )
    tile = lax.all_to_all(tile, ("lat", "lon"), 0, 0, tiled=True)
    new_vec, growth = pl.pallas_call(
        functools.partial(scale_kernel, total),
        out_shape=[jax.ShapeDtypeStruct((rows, chans, cols), F32), jax.ShapeDtypeStruct((1, 128), F32)],
        in_specs=[IN_VMEM, IN_VMEM],
        out_specs=[IN_HBM, IN_VMEM],
        scratch_shapes=[pltpu.VMEM((rows, chans, cols), F32), pltpu.SemaphoreType.DMA((rows,))],
        compiler_params=params(),
        name="scale",
    )(in_vmem(tile), in_vmem(w))
    return jnp.transpose(new_vec, (0, 2, 1)), growth[0, :1]


def solution(mesh):
    in_specs = (
        P(("grp", "lat"), "lon", None),
        P(),
        P(),
        P(),
        P(),
        P(),
        P(None, ("grp", "lat"), "lon", None),
        P(None, ("grp", "lat"), "lon"),
        P(None, ("grp", "lat"), "lon", None),
    )
    out_specs = (P(("grp", "lat"), "lon", None), P("grp"))
    fn = functools.partial(on_device, mesh.shape["lat"], mesh.shape["lon"])
    return jax.shard_map(fn, mesh=mesh, in_specs=in_specs, out_specs=out_specs, check_vma=False)
```

```python
import functools
import math

import jax
import jax.numpy as jnp
import numpy as np
from jax import lax
from jax.experimental import pallas as pl
from jax.experimental.pallas import tpu as pltpu
from jax.sharding import PartitionSpec as P

F32 = jnp.float32
BF16 = jnp.bfloat16
LAT_SPAN = 70.0 * math.pi / 180.0
MARGIN = 8
EARLY = 2
EXT = 16
VMEM = pltpu.VMEM
ACROSS = (((1,), (1,)), ((), ()))
IN_VMEM = pl.BlockSpec(memory_space=pltpu.VMEM)
IN_HBM = pl.BlockSpec(memory_space=pltpu.HBM)
IN_SMEM = pl.BlockSpec(memory_space=pltpu.SMEM)


def in_vmem(x):
    return pltpu.with_memory_space_constraint(x, pltpu.VMEM)


def tap_index(a, b, flipped):
    return (6 - a) * 7 + (6 - b) if flipped else a * 7 + b


def spread_taps(taps_ref, k0, k1):
    for layer in range(taps_ref.shape[2]):

        def low(index):
            return jnp.broadcast_to(taps_ref[index // 7, index % 7, layer : layer + 1, :128], (8, 128))

        def high(index):
            row = taps_ref[index // 7, index % 7, layer : layer + 1, 128:]
            return jnp.broadcast_to(row, (8, row.shape[1]))

        for a in range(7):
            for b in range(7):
                k0[layer, a * 7 + b] = low(a * 7 + b)
                for flipped in (0, 1):
                    pair = [high(tap_index(a, b, flipped)), high(tap_index(6 - a, b, flipped))]
                    k1[layer, flipped, a * 7 + b] = jnp.concatenate(pair, axis=1)


def tap_tile(k0, k1, layer, flipped, rows, out_ref, base, low_window, high_window):
    half = rows // 2
    acc = [None] * rows
    for b in range(7):
        taps = [k0[layer, tap_index(a, b, flipped)] for a in range(7)]
        for r in range(rows):
            x = low_window(r, b)
            for a in range(7):
                o = r + 3 - a
                if 0 <= o < rows:
                    term = taps[a] * x
                    acc[o] = term if acc[o] is None else acc[o] + term
    for o in range(rows):
        out_ref[o, pl.ds(base, 8), :128] = acc[o]
    acc = [None] * half
    for b in range(7):
        taps = [k1[layer, int(flipped), a * 7 + b] for a in range(7)]
        for q in range(half + 3):
            x = high_window(q, b)
            for a in range(7):
                o = q + 3 - a
                if 0 <= o < half:
                    term = taps[a] * x
                    acc[o] = term if acc[o] is None else acc[o] + term
    for o in range(half):
        out_ref[o, pl.ds(base, 8), 128:] = acc[o][:, :64]
        out_ref[rows - 1 - o, pl.ds(base, 8), 128:] = acc[o][:, 64:]


def plane_windows(x0, x1, base):
    return (
        lambda r, b: x0[r, pl.ds(base + (b - 3), 8), :],
        lambda q, b: x1[q, pl.ds(base + (b - 3), 8), :],
    )


def planes_kernel(layer, flipped, f_ref, k0, k1, x0, x1, early_ref):
    rows = f_ref.shape[0]
    half = rows // 2

    def load_row(r):
        return f_ref[r].astype(BF16).astype(F32)

    for q in range(half + 3):
        low, high = load_row(q), load_row(rows - 1 - q)
        if q < half:
            x0[q] = low[:, :128]
            x0[rows - 1 - q] = high[:, :128]
        x1[q] = jnp.concatenate([low[:, 128:], high[:, 128:]], axis=1)

    @pl.loop(0, EARLY)
    def _(j):
        base = pl.multiple_of(j * 8, 8)
        tap_tile(k0, k1, layer, flipped, rows, early_ref, base, *plane_windows(x0, x1, base + 8))


def conv_local(x0, x1, early_ref, lon_ref, k0, k1, layer, out_ref, e0, e1, flipped, beside=None):
    rows, cols, _ = out_ref.shape
    half = rows // 2

    def ends(ref, index, x, side):
        ref[0, index, :MARGIN, :] = side[:MARGIN]
        ref[0, index, MARGIN:, :] = x[index, : 2 * MARGIN, :]
        ref[1, index, : 2 * MARGIN, :] = x[index, cols - 2 * MARGIN :, :]
        ref[1, index, 2 * MARGIN :, :] = side[MARGIN:]

    for r in range(rows):
        ends(e0, r, x0, lon_ref[r, :, :128].astype(F32))
    for q in range(half + 3):
        low, high = lon_ref[q, :, 128:].astype(F32), lon_ref[rows - 1 - q, :, 128:].astype(F32)
        ends(e1, q, x1, jnp.concatenate([low, high], axis=1))

    def both(j, *windows):
        tap_tile(k0, k1, layer, flipped, rows, out_ref, pl.multiple_of(j * 8, 8), *windows)
        if beside is not None:
            beside(j)

    last = cols // 8 - 1

    @pl.loop(0, 2)
    def _(s):
        both(
            s * last,
            lambda r, b: e0[s, r, MARGIN - 3 + b : 2 * MARGIN - 3 + b, :],
            lambda q, b: e1[s, q, MARGIN - 3 + b : 2 * MARGIN - 3 + b, :],
        )

    for r in range(rows):
        out_ref[r, 8 : 8 + 8 * EARLY, :] = early_ref[r]
    if beside is not None:
        for j in range(1, 1 + EARLY):
            beside(j)

    @pl.loop(1 + EARLY, last, unroll=2)
    def _(j):
        both(j, *plane_windows(x0, x1, pl.multiple_of(j * 8, 8)))


def conv_scratch(rows):
    return [
        pltpu.VMEM((2, rows, 3 * MARGIN, 128), F32),
        pltpu.VMEM((2, rows // 2 + 3, 3 * MARGIN, 128), F32),
    ]


def conv_kernel(layer, flipped, x0, x1, early_ref, lon_ref, k0, k1, out_ref, *scratch):
    conv_local(x0, x1, early_ref, lon_ref, k0, k1, layer, out_ref, *scratch, flipped)


def first_conv_kernel(
    area_ref, f_ref, x0, x1, early_ref, lon_ref, k0, k1, turned_ref, slope_hbm, out_ref, sum_ref, normed_out, slope_out, e0, e1, sems
):
    rows, cols, _ = f_ref.shape
    start = lax.axis_index("lat") * rows
    fetches = [
        pltpu.make_async_copy(slope_hbm.at[layer], slope_out.at[layer], sems.at[layer])
        for layer in range(slope_hbm.shape[0])
    ]
    for fetch in fetches:
        fetch.start()
    one = lax.broadcasted_iota(jnp.int32, (cols, cols), 0) == lax.broadcasted_iota(jnp.int32, (cols, cols), 1)
    eye = jnp.where(one, 1.0, 0.0).astype(BF16)

    def turn_row(r):
        x = f_ref[r]
        sum_ref[...] += area_ref[0, start + r] * jnp.sum(x * x, axis=0, keepdims=True)
        for layer in range(turned_ref.shape[0]):
            turned = lax.dot_general(eye, turned_ref[layer, r], ACROSS, preferred_element_type=F32)
            normed_out[layer, r] = turned.astype(BF16)

    sum_ref[...] = jnp.zeros_like(sum_ref)
    steps = cols // 8
    for j in range(steps, rows):
        turn_row(j)

    def beside(j):
        if rows >= steps:
            turn_row(j)
        else:
            pl.when(j < rows)(lambda: turn_row(j))

    conv_local(x0, x1, early_ref, lon_ref, k0, k1, 0, out_ref, e0, e1, False, beside)
    for fetch in fetches:
        fetch.wait()


def place_halo(parity, a_ref, b_ref, h0, h1):
    width = h0.shape[1]
    cols = width - EXT
    middle = cols // 2
    lane = lax.broadcasted_iota(jnp.int32, (width // 2, 128), 1)
    for e in range(3):
        for ref, first in ((a_ref, (1 - parity) * 3), (b_ref, parity * 3)):
            row = ref[e, :width, :].astype(F32)
            h0[first + e, :MARGIN, :] = row[cols : cols + MARGIN]
            h0[first + e, MARGIN : MARGIN + cols, :] = row[:cols]
            h0[first + e, MARGIN + cols :, :] = row[cols + MARGIN :]
        a_up, a_down = a_ref[e, width:, :].astype(F32), a_ref[2 - e, width:, :].astype(F32)
        b_up, b_down = b_ref[e, width:, :].astype(F32), b_ref[2 - e, width:, :].astype(F32)
        up, down = jnp.where(parity == 1, a_up, b_up), jnp.where(parity == 1, b_down, a_down)
        first = jnp.where(lane < 64, up, pltpu.roll(down, 64, 1))
        second = jnp.where(lane < 64, pltpu.roll(up, 64, 1), down)
        h1[e, :MARGIN, :] = first[middle:]
        h1[e, MARGIN : MARGIN + middle, :] = first[:middle]
        h1[e, MARGIN + middle : MARGIN + cols, :] = second[:middle]
        h1[e, MARGIN + cols :, :] = second[middle:]


def conv_halo(h0, h1, acc_ref, k0, k1, layer, edge, flipped):
    rows, cols, _ = acc_ref.shape
    unroll = 2

    def add(acc, index, term):
        acc[index] = term if acc[index] is None else acc[index] + term

    @pl.loop(0, cols // (8 * unroll))
    def _(block):
        bases = [pl.multiple_of(block * (8 * unroll) + 8 * i, 8) for i in range(unroll)]
        acc = [[None] * 6 for _ in bases]
        for b in range(7):
            taps = {a: k0[layer, tap_index(a, b, flipped)] for a in (0, 1, 2, 4, 5, 6)}
            for i, base in enumerate(bases):
                for e in range(3):
                    upper = h0[e, pl.ds(base + (MARGIN - 3 + b), 8), :]
                    for o in range(e + 1):
                        add(acc[i], o, taps[e - o] * upper)
                    lower = h0[3 + e, pl.ds(base + (MARGIN - 3 + b), 8), :]
                    for p in range(e, 3):
                        add(acc[i], 3 + p, taps[6 + e - p] * lower)
        for i, base in enumerate(bases):
            for o in range(6):
                own = o if o < 3 else rows - 6 + o
                edge[o, pl.ds(base, 8), :128] = acc_ref[own, pl.ds(base, 8), :128] + acc[i][o]
        acc = [[None] * 3 for _ in bases]
        for b in range(7):
            taps = [k1[layer, int(flipped), a * 7 + b] for a in range(3)]
            for i, base in enumerate(bases):
                for e in range(3):
                    both = h1[e, pl.ds(base + (MARGIN - 3 + b), 8), :]
                    for o in range(e + 1):
                        add(acc[i], o, taps[e - o] * both)
        for i, base in enumerate(bases):
            for o in range(3):
                edge[o, pl.ds(base, 8), 128:] = acc_ref[o, pl.ds(base, 8), 128:] + acc[i][o][:, :64]
                own = acc_ref[rows - 1 - o, pl.ds(base, 8), 128:]
                edge[5 - o, pl.ds(base, 8), 128:] = own + acc[i][o][:, 64:]


def halo_scratch(cols, chans):
    return [
        pltpu.VMEM((6, cols + 2 * MARGIN, 128), F32),
        pltpu.VMEM((3, cols + 2 * MARGIN, 128), F32),
        pltpu.VMEM((6, cols, chans), F32),
    ]


def wide(inv, chans):
    return jnp.concatenate([inv, inv[:, : chans - 128]], axis=1)


def project(y, normed, inv):
    chans = y.shape[1]
    normal = normed.astype(F32)
    first = jnp.sum(y, axis=1, keepdims=True) * (1.0 / chans)
    second = jnp.sum(normal * y, axis=1, keepdims=True) * (1.0 / chans)
    return inv * (y - first - normal * second)


def forward_net(y, normed, inv, slope, gain, w_in, w_out_turned, scale):
    operand = (gain * project(y, normed, inv)).astype(BF16)
    hidden = jnp.dot(operand, w_in, preferred_element_type=F32)
    gated = (slope.astype(F32) * hidden).astype(BF16)
    return scale * lax.dot_general(gated, w_out_turned, ACROSS, preferred_element_type=F32)


def adjoint_net(g, normed, inv, slope, gain, w_in, w_out_turned, scale):
    scaled = (scale * g).astype(BF16)
    hidden = jnp.dot(scaled, w_out_turned, preferred_element_type=F32)
    gated = (slope.astype(F32) * hidden).astype(BF16)
    back = lax.dot_general(gated, w_in, ACROSS, preferred_element_type=F32)
    return project(gain * back, normed, inv).astype(BF16)


def fold(values):
    count = values.shape[0] // 2
    return jnp.concatenate([values[:count], values[count:]], axis=1)


def send_rows(parity, field, lon_ref, a_ref, b_ref):
    rows, cols = field.shape[0], field.shape[1]
    width = cols + EXT
    for e in range(3):
        for ref, row in ((a_ref, (1 - parity) * (rows - 3) + e), (b_ref, parity * (rows - 3) + e)):
            ref[e, :cols, :] = field[row, :, :128].astype(BF16)
            ref[e, width : width + cols // 2, :] = fold(field[row, :, 128:].astype(F32)).astype(BF16)
    for r in range(rows):
        lon_ref[r, :MARGIN, :] = field[r, cols - MARGIN :, :].astype(BF16)
        lon_ref[r, MARGIN:, :] = field[r, :MARGIN, :].astype(BF16)


def flat(x):
    return x.reshape(x.shape[0] * x.shape[1], x.shape[2])


class Rows:
    def __init__(self, rows, outer):
        self.spans = [(0, 3), (rows - 3, 3)] if outer else [(3, rows - 6)]

    def get(self, ref, *lead):
        return jnp.concatenate([flat(ref[(*lead, slice(a, a + n))]) for a, n in self.spans], axis=0)

    def put(self, ref, value):
        cols, done = ref.shape[1], 0
        for a, n in self.spans:
            ref[a : a + n] = value[done * cols : (done + n) * cols].reshape(n, cols, value.shape[1])
            done += n

    def numbers(self):
        return [a + i for a, n in self.spans for i in range(n)]


def both_blocks(acc_ref, edge, fn):
    rows = acc_ref.shape[0]
    inner, outer = Rows(rows, False), Rows(rows, True)
    fn(outer, flat(edge[...]))
    fn(inner, inner.get(acc_ref))


def net_operands(layer, block, refs):
    normed_ref, inv_ref, slope_ref, gain_ref, win_ref, wout_ref, scale_ref = refs
    return [
        block.get(normed_ref, layer), wide(block.get(inv_ref, layer), normed_ref.shape[3]), block.get(slope_ref, layer),
        gain_ref[layer : layer + 1, :], win_ref[layer], wout_ref[layer], scale_ref[layer : layer + 1, :],
    ]


def tangent_kernel(layer, last, area_ref, acc_ref, a_ref, b_ref, k0, k1, t_ref, *rest):
    net, rest = rest[:7], rest[7:]
    rows, cols, chans = acc_ref.shape
    lat = lax.axis_index("lat")
    if last:
        g_ref, db_ref, sum_ref, lon_ref, sa_ref, sb_ref, h0, h1, edge = rest
        sum_ref[...] = jnp.zeros_like(sum_ref)
    else:
        t_out, lon_ref, sa_ref, sb_ref, h0, h1, edge = rest
    place_halo(lat % 2, a_ref, b_ref, h0, h1)
    conv_halo(h0, h1, acc_ref, k0, k1, layer, edge, False)

    def work(block, y):
        operands = net_operands(layer, block, net)
        t = block.get(t_ref) + forward_net(y, *operands)
        if not last:
            block.put(t_out, t)
            return
        parts = []
        for i, r in enumerate(block.numbers()):
            u = t[i * cols : (i + 1) * cols]
            g = area_ref[0, lat * rows + r] * u
            sum_ref[...] += jnp.sum(g * u, axis=0, keepdims=True)
            parts.append(g)
        g = jnp.concatenate(parts, axis=0)
        block.put(g_ref, g)
        block.put(db_ref, adjoint_net(g, *operands))

    both_blocks(acc_ref, edge, work)
    send_rows(lat % 2, db_ref if last else t_out, lon_ref, sa_ref, sb_ref)


def adjoint_kernel(layer, acc_ref, a_ref, b_ref, k0, k1, g_ref, *rest):
    net, (g_out, db_ref, lon_ref, sa_ref, sb_ref, h0, h1, edge) = rest[:7], rest[7:]
    parity = lax.axis_index("lat") % 2
    place_halo(parity, a_ref, b_ref, h0, h1)
    conv_halo(h0, h1, acc_ref, k0, k1, layer + 1, edge, True)

    def work(block, y):
        g = block.get(g_ref) + y
        block.put(g_out, g)
        block.put(db_ref, adjoint_net(g, *net_operands(layer, block, net)))

    both_blocks(acc_ref, edge, work)
    send_rows(parity, db_ref, lon_ref, sa_ref, sb_ref)


def final_kernel(
    area_ref, acc_ref, a_ref, b_ref, k0, k1, g_ref, vv_ref, uu_ref, w_ref, tile_ref, h0, h1, edge, ww
):
    rows = acc_ref.shape[0]
    lat = lax.axis_index("lat")
    place_halo(lat % 2, a_ref, b_ref, h0, h1)
    conv_halo(h0, h1, acc_ref, k0, k1, 0, edge, True)
    ww[...] = jnp.zeros_like(ww)

    def row(r, y):
        g = g_ref[r] + y
        w = g * area_ref[1, lat * rows + r]
        w_ref[r] = jnp.transpose(w)
        ww[...] += jnp.sum(g * w, axis=0, keepdims=True)

    for e in range(3):
        row(e, edge[e])
        row(rows - 3 + e, edge[3 + e])

    for r in range(3, rows - 3):
        row(r, acc_ref[r])

    which = lax.broadcasted_iota(jnp.int32, (1, 128), 1)
    vv, uu, wv = (jnp.sum(ref[...]) for ref in (vv_ref, uu_ref, ww))
    tile = jnp.where(which == 0, vv, jnp.where(which == 1, uu, jnp.where(which == 2, wv, 0.0)))
    for i in range(tile_ref.shape[0]):
        tile_ref[i] = tile


def scale_kernel(total, tile_ref, w_ref, out_hbm, growth_ref, scaled, sems):
    sums = jnp.sum(tile_ref[...], axis=0) * (1.0 / total)
    vv, uu, ww = (jnp.broadcast_to(sums[:, i : i + 1], (1, 128)) for i in range(3))
    growth_ref[...] = jnp.sqrt(uu / (vv + 1e-06))
    factor = 1.0 / jnp.sqrt(ww + 1e-06)
    copies = []
    for r in range(w_ref.shape[0]):
        scaled[r] = w_ref[r] * factor
        copies.append(pltpu.make_async_copy(scaled.at[r], out_hbm.at[r], sems.at[r]))
        copies[-1].start()
    for copy in copies:
        copy.wait()


def extend_kernel(after_ref, lon_ref, sa_in, sb_in, sa_ref, sb_ref):
    rows, width = lon_ref.shape[0], sa_ref.shape[1] // 3 * 2
    cols = width - EXT
    parity = lax.axis_index("lat") % 2
    for e in range(3):
        for source, ref, row in (
            (sa_in, sa_ref, (1 - parity) * (rows - 3) + e), (sb_in, sb_ref, parity * (rows - 3) + e)
        ):
            ref[e, :cols, :] = source[e, :cols, :]
            ref[e, width : width + cols // 2, :] = source[e, width : width + cols // 2, :]
            side = lon_ref[row]
            ref[e, cols:width, :] = side[:, :128]
            ref[e, width + cols // 2 :, :] = fold(side[:, 128:].astype(F32)).astype(BF16)


def edges_kernel(
    turned_hbm, taps_hbm, inv_hbm, t_ref, lon_ref, sa_ref, sb_ref, k0, k1, inv_out, turned, taps_ref, inv_ref, sems
):
    rows = turned.shape[0]
    copies = [pltpu.make_async_copy(turned_hbm.at[r], turned.at[r], sems.at[r]) for r in range(rows)]
    small = [
        pltpu.make_async_copy(inv_hbm, inv_ref, sems.at[rows]),
        pltpu.make_async_copy(taps_hbm, taps_ref, sems.at[rows + 1]),
    ]
    for copy in small + copies:
        copy.start()
    for copy in small:
        copy.wait()
    spread_taps(taps_ref, k0, k1)
    for layer in range(inv_ref.shape[0]):
        for r in range(rows):
            inv = jnp.broadcast_to(inv_ref[layer, r : r + 1, :], (128, inv_ref.shape[2]))
            inv_out[layer, r] = jnp.transpose(inv)
    for r, copy in enumerate(copies):
        copy.wait()
        t_ref[r] = jnp.transpose(turned[r])
    send_rows(lax.axis_index("lat") % 2, t_ref, lon_ref, sa_ref, sb_ref)


def params():
    return pltpu.CompilerParams(vmem_limit_bytes=16 * 1024 * 1024)


def on_device(lat_size, lon_size, perturb, kernels, gains, w_in, w_out, scales, normed, inv_std, slope):
    rows, cols, chans = perturb.shape
    hidden = w_in.shape[2]
    layers = kernels.shape[0]
    lat_total = rows * lat_size
    angles = LAT_SPAN * (np.arange(lat_total) + 0.5) / lat_total
    total = float(np.sum(np.cos(angles))) * cols * lon_size * chans
    table = np.stack([np.cos(angles), 1.0 / np.cos(angles)]).astype(np.float32)
    area = jnp.asarray(table)
    across_cells = jnp.transpose(w_out, (0, 2, 1))
    swap_a = [(i, i ^ 1) for i in range(lat_size) if i ^ 1 < lat_size]
    swap_b = [pair for i in range(1, lat_size - 1, 2) for pair in ((i, i + 1), (i + 1, i))]
    swap_lon = [(i, (i + 1) % lon_size) for i in range(lon_size)]

    lon_shape = VMEM((rows, EXT, chans), BF16)
    send_shape = VMEM((3, (cols + EXT) // 2 * 3, 128), BF16)
    full32 = VMEM((rows, cols, chans), F32)
    full16 = VMEM((rows, cols, chans), BF16)
    sums = VMEM((1, chans), F32)

    def call(kernel, out_shape, in_specs, args, scratch=(), flops=0, name=None):
        args = [pltpu.with_memory_space_constraint(x, spec.memory_space) if spec is not IN_SMEM else x for spec, x in zip(in_specs, args)]
        return pl.pallas_call(
            kernel,
            out_shape=out_shape,
            in_specs=in_specs,
            out_specs=[IN_VMEM] * len(out_shape),
            scratch_shapes=list(scratch),
            compiler_params=params(),
            cost_estimate=pl.CostEstimate(flops=flops, bytes_accessed=4_000_000, transcendentals=0),
            name=name,
        )(*args)

    def exchange(layer, flipped, field, lon, send_a, send_b):
        side = lax.ppermute(lon, "lon", swap_lon)
        planes = call(
            functools.partial(planes_kernel, layer, flipped),
            [
                VMEM((rows, cols, 128), F32), VMEM((rows // 2 + 3, cols, 128), F32),
                VMEM((rows, 8 * EARLY, chans), F32),
            ],
            [IN_VMEM] * 3, (field, k0, k1),
            flops=conv_flops // 8, name="planes",
        )
        send_a, send_b = call(
            extend_kernel, [send_shape] * 2, [IN_VMEM] * 4, (planes[2], side, send_a, send_b), name="extend"
        )
        halo_b = lax.ppermute(send_b, "lat", swap_b)
        halo_a = lax.ppermute(send_a, "lat", swap_a)
        return (*planes, side), halo_a, halo_b

    conv_flops = 2 * 49 * rows * cols * chans
    net_flops = 4 * rows * cols * chans * hidden
    kscr = conv_scratch(rows)
    hscr = halo_scratch(cols, chans)

    tangent, lon, send_a, send_b, k0, k1, inv_cells = call(
        edges_kernel,
        [
            full32, lon_shape, send_shape, send_shape, VMEM((layers, 49, 8, 128), F32),
            VMEM((layers, 2, 49, 8, 128), F32), VMEM((layers, rows, cols, 128), F32),
        ],
        [IN_HBM] * 3, (jnp.transpose(perturb, (0, 2, 1)), jnp.transpose(kernels, (1, 2, 0, 3)), inv_std),
        [
            pltpu.VMEM((rows, chans, cols), F32), pltpu.VMEM((7, 7, layers, chans), F32),
            pltpu.VMEM(inv_std.shape, F32), pltpu.SemaphoreType.DMA((rows + 2,)),
        ],
        name="edges",
    )
    taken, halo_a, halo_b = exchange(0, False, tangent, lon, send_a, send_b)
    acc, vv, normed_cells, slope_cells = call(
        first_conv_kernel,
        [full32, sums, VMEM((layers, rows, cols, chans), BF16), VMEM(slope.shape, BF16)],
        [IN_SMEM] + [IN_VMEM] * 8 + [IN_HBM],
        (area, tangent, *taken, k0, k1, jnp.transpose(normed, (0, 1, 3, 2)), slope),
        kscr + [pltpu.SemaphoreType.DMA((layers,))], conv_flops, "conv_first",
    )
    net = (normed_cells, inv_cells, slope_cells, gains, w_in, across_cells, scales)
    for layer in range(layers):
        last = layer == layers - 1
        outs = [full32, full16, sums] if last else [full32]
        outs = outs + [lon_shape, send_shape, send_shape]
        got = call(
            functools.partial(tangent_kernel, layer, last), outs, [IN_SMEM] + [IN_VMEM] * 13,
            (area, acc, halo_a, halo_b, k0, k1, tangent) + net, hscr, net_flops, f"tangent{layer}",
        )
        if last:
            grad, back, uu = got[:3]
        else:
            tangent = got[0]
        taken, halo_a, halo_b = exchange(layer + (not last), last, back if last else tangent, *got[-3:])
        if not last:
            (acc,) = call(
                functools.partial(conv_kernel, layer + 1, False), [full32], [IN_VMEM] * 6, (*taken, k0, k1),
                kscr, conv_flops, f"conv{layer + 1}",
            )
    for layer in range(layers - 1, -1, -1):
        (acc,) = call(
            functools.partial(conv_kernel, layer, True), [full32], [IN_VMEM] * 6, (*taken, k0, k1),
            kscr, conv_flops, f"convt{layer}",
        )
        if layer > 0:
            grad, back, lon, send_a, send_b = call(
                functools.partial(adjoint_kernel, layer - 1), [full32, full16, lon_shape, send_shape, send_shape],
                [IN_VMEM] * 13, (acc, halo_a, halo_b, k0, k1, grad) + net, hscr, net_flops, f"adjoint{layer - 1}",
            )
            taken, halo_a, halo_b = exchange(layer - 1, True, back, lon, send_a, send_b)
    members = lat_size * lon_size
    w, tile = call(
        final_kernel, [VMEM((rows, chans, cols), F32), VMEM((members, 1, 128), F32)], [IN_SMEM] + [IN_VMEM] * 8,
        (area, acc, halo_a, halo_b, k0, k1, grad, vv, uu), hscr + [pltpu.VMEM((1, chans), F32)], 0, "final",
    )
    tile = lax.all_to_all(tile, ("lat", "lon"), 0, 0, tiled=True)
    new_vec, growth = pl.pallas_call(
        functools.partial(scale_kernel, total),
        out_shape=[jax.ShapeDtypeStruct((rows, chans, cols), F32), jax.ShapeDtypeStruct((1, 128), F32)],
        in_specs=[IN_VMEM, IN_VMEM],
        out_specs=[IN_HBM, IN_VMEM],
        scratch_shapes=[pltpu.VMEM((rows, chans, cols), F32), pltpu.SemaphoreType.DMA((rows,))],
        compiler_params=params(),
        name="scale",
    )(in_vmem(tile), in_vmem(w))
    return jnp.transpose(new_vec, (0, 2, 1)), growth[0, :1]


def solution(mesh):
    in_specs = (
        P(("grp", "lat"), "lon", None),
        P(),
        P(),
        P(),
        P(),
        P(),
        P(None, ("grp", "lat"), "lon", None),
        P(None, ("grp", "lat"), "lon"),
        P(None, ("grp", "lat"), "lon", None),
    )
    out_specs = (P(("grp", "lat"), "lon", None), P("grp"))
    fn = functools.partial(on_device, mesh.shape["lat"], mesh.shape["lon"])
    return jax.shard_map(fn, mesh=mesh, in_specs=in_specs, out_specs=out_specs, check_vma=False)
```
